32 devices in a mesh: groups: 1, tm: 32 (over z, y, x, core).
Axes of the slice: x: 2, y: 2, z: 4, core: 2. Of those that a mesh axis runs over, the one named last changes fastest.
Arguments:
- latents: bfloat16 [32, 512, 512], P(('groups', 'tm')), may hold values from -21 to 21
- w_query: bfloat16 [512, 512], replicated, may hold values from -3 to 3
- w_key: bfloat16 [512, 512], replicated, may hold values from -3 to 3
- w_value: bfloat16 [512, 512], replicated, may hold values from -0.25 to 0.25
- w_out: bfloat16 [512, 512], replicated, may hold values from -0.25 to 0.25
- w_time: bfloat16 [3, 512, 512], replicated, may hold values from -0.15625 to 0.15625
- w_space: bfloat16 [3, 3, 512, 512], replicated, may hold values from -0.09375 to 0.09375
- tile_starts: int32 [4], P('groups'), may hold values from 0 to 25, as said below
Outputs:
- decoded: bfloat16 [32, 512, 512], P(('groups', 'tm'))
The draws below stay inside these ranges and needn't reach their ends.
Inputs may be any that keep to these rules, and one draw needn't show every extreme that they name: `tile_starts`: Increasing; the first is 0, the last is (3) * 8 + 1, and every other start t lies within 2 frames of t * 8.
All inputs are finite; a program needn't handle non-finite values.
Results may differ from the reference program's by a relative error of at most 0.0096.
Values may be sent and summed in bfloat16 or wider, within the bound.
A program may use at most 64 MiB of HBM per device.

```python
import math
import jax
import jax.numpy as jnp
from jax import lax

C = 512
PH = 16
PW = 32
TILE = 8
OV = 2
FRAMES = 32
POS = 512
NT = 4


def draw_latents(key, part):
    base_key = jax.random.fold_in(key, 21)
    keys = jax.random.split(base_key, 3)
    column = jnp.exp(jax.random.uniform(keys[0], (C,), jnp.float32, math.log(0.3), math.log(3.0)))
    rowwise = jnp.exp(jax.random.uniform(keys[1], (FRAMES, POS, 1), jnp.float32, math.log(0.5), math.log(2.0)))
    raw = jax.random.truncated_normal(keys[2], -3.0, 3.0, (FRAMES, POS, C), jnp.float32)
    scaled = raw * column * rowwise
    return scaled.astype(jnp.bfloat16)


def shared_query(key):
    raw = jax.random.truncated_normal(jax.random.fold_in(key, 31), -4.0, 4.0, (C, C), jnp.float32)
    return raw * C ** (-0.5)


def draw_w_query(key, part):
    return shared_query(key).astype(jnp.bfloat16)


def draw_w_key(key, part):
    raw = jax.random.truncated_normal(jax.random.fold_in(key, 32), -4.0, 4.0, (C, C), jnp.float32)
    return (raw * C ** (-0.5)).astype(jnp.bfloat16)


def draw_tile_starts(key, part):
    index = jnp.arange(NT).astype(jnp.int32)
    jitter = jax.random.randint(jax.random.fold_in(key, 41), (NT,), -2, 3).astype(jnp.int32)
    starts = index * TILE + jitter
    starts = jnp.where(index == NT - 1, index * TILE + 1, starts)
    starts = jnp.where(index == 0, 0, starts)
    return starts.astype(jnp.int32)


def normal_values(key, dims, width, most, held_as=jnp.bfloat16):
    drawn = jax.random.normal(key, dims, jnp.float32) * width
    return jnp.minimum(jnp.maximum(drawn, -most), most).astype(held_as)


def setup_inputs(seed: int = 0, part: int = 0) -> dict:
    key_list = jax.random.split(jax.random.key(seed), 9)
    part_keys = jax.random.split(jax.random.fold_in(key_list[8], part), 9)
    return {
        "latents": draw_latents(jax.random.fold_in(jax.random.fold_in(key_list[8], part), 71), part),
        "w_query": draw_w_query(jax.random.fold_in(key_list[8], 71), part),
        "w_key": draw_w_key(jax.random.fold_in(key_list[8], 71), part),
        "w_value": normal_values(key_list[3], (C, C), C ** -0.5, 0.25),
        "w_out": normal_values(key_list[4], (C, C), C ** -0.5, 0.25),
        "w_time": normal_values(key_list[5], (3, C, C), (3 * C) ** -0.5, 0.15625),
        "w_space": normal_values(key_list[6], (3, 3, C, C), (9 * C) ** -0.5, 0.09375),
        "tile_starts": draw_tile_starts(jax.random.fold_in(jax.random.fold_in(key_list[8], part), 71), part),
    }


epsilon = 1e-06

def rms_norm(array):
    wide = array.astype(jnp.float32)
    return (wide * lax.rsqrt(lax.optimization_barrier(jnp.mean(wide * wide, axis=-1, keepdims=True)) + epsilon)).astype(jnp.bfloat16)

def project(array, weight):
    extent = array.shape
    product = jnp.dot(array.reshape(-1, extent[-1]), weight, preferred_element_type=jnp.float32)
    return product.reshape(extent[:-1] + (weight.shape[-1],))

def tile_frames(frames, starts):
    reached = starts[None, :] <= frames[:, None]
    new_start = lax.optimization_barrier(jnp.max(jnp.where(reached, starts[None, :], 0), axis=1)).astype(jnp.int32)
    earlier = starts[None, :] < new_start[:, None]
    old_start = lax.optimization_barrier(jnp.max(jnp.where(earlier, starts[None, :], 0), axis=1)).astype(jnp.int32)
    inside = frames - new_start
    shared = jnp.logical_and(new_start > 0, inside < OV)
    fade = jnp.where(shared, (inside + 1).astype(jnp.float32) / float(OV + 1), jnp.float32(1.0))
    return (new_start, old_start, fade.astype(jnp.float32)[:, None, None])

def space_mix(blended, w_space):
    length = blended.shape[0]
    channels = blended.shape[-1]
    spatial = blended.reshape(length, PH, PW, channels)
    padded = jnp.pad(spatial, ((0, 0), (1, 1), (1, 1), (0, 0)))
    summed = jnp.zeros((length * PH * PW, channels), jnp.float32)
    for row_shift in range(3):
        for col_shift in range(3):
            window = padded[:, row_shift:row_shift + PH, col_shift:col_shift + PW].reshape(-1, channels)
            summed = summed + jnp.dot(window, w_space[row_shift, col_shift], preferred_element_type=jnp.float32)
    return summed.reshape(length, PH * PW, channels)

def reference(latents, w_query, w_key, w_value, w_out, w_time, w_space, tile_starts):
    normed = rms_norm(latents)
    queries = project(normed, w_query).astype(jnp.bfloat16)
    key_rows = project(normed, w_key).astype(jnp.bfloat16)
    values = project(normed, w_value).astype(jnp.bfloat16)
    scores = jnp.einsum('fpc,gpc->pfg', queries.astype(jnp.float32), key_rows.astype(jnp.float32)) * C ** (-0.5)
    order = jnp.arange(FRAMES)
    causal = order[:, None] >= order[None, :]
    scores = jnp.where(causal[None], scores, jnp.float32(-1e+30))
    peak = lax.optimization_barrier(jnp.max(scores, axis=-1, keepdims=True))
    expo = jnp.exp(scores - peak)
    weights = (expo / lax.optimization_barrier(jnp.sum(expo, axis=-1, keepdims=True))).astype(jnp.bfloat16)
    attended = jnp.einsum('pfg,gpc->fpc', weights.astype(jnp.float32), values.astype(jnp.float32)).astype(jnp.bfloat16)
    hidden = (latents.astype(jnp.float32) + project(attended, w_out)).astype(jnp.bfloat16)
    smooth = rms_norm(hidden)
    frames = jnp.arange(FRAMES).astype(jnp.int32)
    new_start, old_start, fade = tile_frames(frames, tile_starts)

    def mixed(context):
        summed = jnp.zeros(smooth.shape, jnp.float32)
        for lag_index in range(3):
            source = jnp.maximum(frames - lag_index, context).astype(jnp.int32)
            summed = summed + project(jnp.take(smooth, source, axis=0), w_time[lag_index])
        return summed
    blended = (fade * jax.nn.silu(mixed(new_start)) + (1.0 - fade) * jax.nn.silu(mixed(old_start))).astype(jnp.bfloat16)
    return (hidden.astype(jnp.float32) + space_mix(blended, w_space)).astype(jnp.bfloat16)
```

```python
import functools

import jax
import jax.numpy as jnp
from jax import lax
from jax.experimental import pallas as pl
from jax.experimental.pallas import tpu as pltpu
from jax.sharding import PartitionSpec as P

PH = 16
PW = 32
OV = 2


epsilon = 1e-06


def passed_along(block, axis, distance):
    devices = range(lax.axis_size(axis))
    route = [(i - distance, i) for i in devices if i - distance in devices]
    return lax.ppermute(block, axis, route)


def rms_norm(array):
    wide = array.astype(jnp.float32)
    return (wide * lax.rsqrt(jnp.mean(wide * wide, axis=-1, keepdims=True) + epsilon)).astype(
        jnp.bfloat16
    )


def project(array, weight):
    extent = array.shape
    product = jnp.dot(array.reshape(-1, extent[-1]), weight, preferred_element_type=jnp.float32)
    return product.reshape(extent[:-1] + (weight.shape[-1],))


def tile_frames(frames, starts):
    reached = starts[None, :] <= frames[:, None]
    new_start = jnp.max(jnp.where(reached, starts[None, :], 0), axis=1)
    earlier = starts[None, :] < new_start[:, None]
    old_start = jnp.max(jnp.where(earlier, starts[None, :], 0), axis=1)
    inside = frames - new_start
    shared = jnp.logical_and(new_start > 0, inside < OV)
    fade = jnp.where(shared, (inside + 1).astype(jnp.float32) / float(OV + 1), jnp.float32(1.0))
    return (new_start, old_start, fade[:, None, None])


def attend(triple):
    queries, key_rows, values = triple
    length = queries.shape[0]
    scale = queries.shape[-1] ** (-0.5)
    scores = (
        jnp.einsum("fipc,gipc->ipfg", queries, key_rows, preferred_element_type=jnp.float32) * scale
    )
    order = jnp.arange(length)
    causal = order[:, None] >= order[None, :]
    scores = jnp.where(causal[None, None], scores, jnp.float32(-1e30))
    peak = jnp.max(scores, axis=-1, keepdims=True)
    expo = jnp.exp(scores - peak)
    weights = (expo / jnp.sum(expo, axis=-1, keepdims=True)).astype(jnp.bfloat16)
    return jnp.einsum(
        "ipfg,gipc->fipc", weights, values, preferred_element_type=jnp.float32
    ).astype(jnp.bfloat16)


def time_blend(padded, frames, starts, w_time):
    length = frames.shape[0]
    extent = padded.shape
    channels = extent[-1]
    flattened = padded.reshape(-1, channels)
    products = [
        jnp.dot(flattened, w_time[lag_index], preferred_element_type=jnp.float32).reshape(
            extent[0], -1, channels
        )
        for lag_index in range(3)
    ]
    new_start, old_start, fade = tile_frames(frames, starts)

    def mixed(context):
        summed = jnp.zeros((length,) + products[0].shape[1:], jnp.float32)
        for lag_index in range(3):
            actual = jnp.minimum(lag_index, frames - context)
            for delta_back in range(lag_index + 1):
                chosen = (actual == delta_back).astype(jnp.float32)[:, None, None]
                summed = (
                    summed + chosen * products[lag_index][2 - delta_back : 2 - delta_back + length]
                )
        return summed

    blended = fade * jax.nn.silu(mixed(new_start)) + (1.0 - fade) * jax.nn.silu(mixed(old_start))
    return blended.astype(jnp.bfloat16)


def space_mix(blended, hidden, w_space):
    length = blended.shape[0]
    channels = blended.shape[-1]
    spatial = blended.reshape(length, PH, PW, channels)
    padded = jnp.pad(spatial, ((0, 0), (1, 1), (1, 1), (0, 0)))
    summed = hidden.reshape(-1, channels).astype(jnp.float32)
    for row_shift in range(3):
        for col_shift in range(3):
            window = padded[:, row_shift : row_shift + PH, col_shift : col_shift + PW].reshape(
                -1, channels
            )
            summed = summed + jnp.dot(
                window, w_space[row_shift, col_shift], preferred_element_type=jnp.float32
            )
    return summed.reshape(length, PH * PW, channels).astype(jnp.bfloat16)


def body(latents, w_query, w_key, w_value, w_out, w_time, w_space, tile_starts):
    frames_dev, row_count, channels = latents.shape
    devices_tm = lax.axis_size("tm")
    share = row_count // devices_tm
    normed = rms_norm(latents).reshape(frames_dev, devices_tm, share, channels)
    queries = project(normed, w_query).astype(jnp.bfloat16)
    key_rows = project(normed, w_key).astype(jnp.bfloat16)
    values = project(normed, w_value).astype(jnp.bfloat16)
    attended = attend(
        (
            lax.all_to_all(queries, "tm", split_axis=1, concat_axis=0, tiled=True),
            lax.all_to_all(key_rows, "tm", split_axis=1, concat_axis=0, tiled=True),
            lax.all_to_all(values, "tm", split_axis=1, concat_axis=0, tiled=True),
        )
    )
    attended = lax.all_to_all(attended, "tm", split_axis=0, concat_axis=1, tiled=True).reshape(
        frames_dev, row_count, channels
    )
    hidden = (latents.astype(jnp.float32) + project(attended, w_out)).astype(jnp.bfloat16)
    smooth = rms_norm(hidden)
    reach = (frames_dev + 1) // frames_dev
    pieces = [passed_along(smooth, "tm", stride) for stride in range(reach, 0, -1)]
    earlier = jnp.concatenate(pieces, axis=0)
    offset = lax.axis_index("tm") * frames_dev
    frames = offset + jnp.arange(frames_dev)
    blended = time_blend(jnp.concatenate([earlier, smooth], axis=0), frames, tile_starts, w_time)
    return space_mix(blended, hidden, w_space)


BS = 4
BLOCK = BS * BS
CHUNKS = 4


def iota(shape, dim):
    return lax.broadcasted_iota(jnp.int32, shape, dim)


def one_hot(target, columns):
    rows = target.shape[0]
    return (jnp.broadcast_to(target, (rows, columns)) == iota((rows, columns), 1)).astype(
        jnp.float32
    ).astype(jnp.bfloat16)


def matmul(left, right):
    return jnp.dot(left, right, preferred_element_type=jnp.float32)


def place_of(device):
    core, x, y, z = device % 2, (device // 2) % 2, (device // 4) % 2, device // 8
    return 2 * y + (x + y) % 2, 2 * z + core


def device_at(row, column):
    y = row // 2
    return (column // 2) * 8 + y * 4 + ((row % 2 + y) % 2) * 2 + column % 2


def window_position():
    r = iota((PH * PW, 1), 0)
    device, q = r >> 4, r & 15
    core, x, y, z = device & 1, (device >> 1) & 1, (device >> 2) & 1, device >> 3
    row, column = 2 * y + (x ^ y), 2 * z + core
    return (row * BS + (q >> 2)) * PW + column * BS + (q & 3)


def block_position():
    p = iota((PH * PW, 1), 0)
    py, px = p >> 5, p & 31
    row, column = py >> 2, px >> 2
    y = row >> 1
    device = (column >> 1) * 8 + y * 4 + ((row & 1) ^ y) * 2 + (column & 1)
    return device * BLOCK + (py & 3) * BS + (px & 3)


def normalized(wide):
    scale = lax.rsqrt(jnp.mean(wide * wide, axis=-1, keepdims=True) + epsilon)
    return (wide * scale).astype(jnp.bfloat16)


def silu(v):
    return v / (1.0 + jnp.exp(-v))


def block_kernel(
    starts,
    latents_any,
    wq_any,
    wk_any,
    wv_any,
    wo_any,
    wt_any,
    ws_any,
    returned,
    latents,
    wqkv,
    wo,
    wt,
    ws,
    outgoing,
    arrived,
    keys,
    values,
    lag1,
    lag2,
    ext,
    kept,
    back,
    weight_sem,
    sent,
    got,
    halo_sent,
    halo_got,
    back_sent,
    back_got,
    own_sem,
    *,
    n,
):
    channels = latents.shape[-1]
    chunk = n // CHUNKS
    rows = chunk * BLOCK
    me = lax.axis_index("tm")
    plane, local = me // chunk, me % chunk
    mesh_id = pl.DeviceIdType.MESH

    barrier = pltpu.get_barrier_semaphore()

    @pl.loop(1, n)
    def _(k):
        pl.semaphore_signal(
            barrier, inc=1, device_id={"tm": (me + k) % n}, device_id_type=mesh_id
        )

    fetch = pltpu.make_async_copy(latents_any.at[0], latents, weight_sem.at[6])
    fetch.start()
    weights = [
        pltpu.make_async_copy(source, target, weight_sem.at[i])
        for i, (source, target) in enumerate(
            (
                (wq_any, wqkv.at[:, :channels]),
                (wk_any, wqkv.at[:, channels : 2 * channels]),
                (wv_any, wqkv.at[:, 2 * channels :]),
                (wo_any, wo),
                (wt_any, wt),
                (ws_any, ws),
            )
        )
    ]
    for copy in weights:
        copy.start()

    to_blocks = one_hot(window_position(), PH * PW)
    fetch.wait()
    outgoing[...] = matmul(to_blocks, latents[...]).astype(jnp.bfloat16).reshape(n, BLOCK, channels)
    arrived[me] = outgoing[me]
    pl.semaphore_wait(barrier, n - 1)

    def in_copy(source, target):
        return pltpu.make_async_remote_copy(
            src_ref=outgoing.at[target],
            dst_ref=arrived.at[source],
            send_sem=sent.at[target],
            recv_sem=got.at[source],
            device_id={"tm": target},
            device_id_type=mesh_id,
        )

    def pick(options):
        r = options[0]
        for i in (1, 2, 3):
            r = jnp.where(plane >= i, options[i], r)
        return r

    table = ((0, 1, 2, 3), (1, 0, 3, 2), (2, 2, 1, 1), (3, 3, 0, 0))
    planes = [pick(t) for t in table]

    def go(j, i):
        target = planes[j] * chunk + (local + i) % chunk
        if i == 0:
            @pl.when(target != me)
            def _():
                in_copy(me, target).start()
        else:
            in_copy(me, target).start()
    for j in range(4):
        for i in range(chunk):
            go(j, i)

    row, column = place_of(me)
    edge = jnp.zeros((BS + 2, chunk, channels), jnp.bfloat16)

    @pl.when(row == 0)
    def _():
        for c in range(CHUNKS):
            ext[c, 0] = edge

    @pl.when(row == PH // BS - 1)
    def _():
        for c in range(CHUNKS):
            ext[c, BS + 1] = edge

    @pl.when(column == 0)
    def _():
        for c in range(CHUNKS):
            for i in range(BS + 2):
                ext[c, i, 0] = edge[0]

    @pl.when(column == PW // BS - 1)
    def _():
        for c in range(CHUNKS):
            for i in range(BS + 2):
                ext[c, i, BS + 1] = edge[0]

    lag1[:BLOCK] = jnp.zeros((BLOCK, channels), jnp.float32)
    lag2[: 2 * BLOCK] = jnp.zeros((2 * BLOCK, channels), jnp.float32)

    flat = iota((rows, 1), 0)
    by_position = one_hot((flat % chunk) * BLOCK + flat // chunk, rows)
    by_frame = one_hot((flat % BLOCK) * chunk + flat // BLOCK, rows)

    def wait_plane(c):
        @pl.loop(c * chunk, (c + 1) * chunk)
        def _(source):
            @pl.when(source != me)
            def _():
                in_copy(source, me).wait_recv()

    def blend(c):
        low, high = c * rows, (c + 1) * rows
        held = arrived[c * chunk : (c + 1) * chunk].reshape(rows, channels).astype(jnp.float32)
        normed = normalized(held)
        if c == 0:
            for copy in weights[:3]:
                copy.wait()
        projected = matmul(normed, wqkv[...]).astype(jnp.bfloat16)
        queries = projected[:, :channels]
        keys[low:high] = projected[:, channels : 2 * channels]
        values[low:high] = projected[:, 2 * channels :]
        scores = lax.dot_general(
            queries,
            keys[:high],
            (((1,), (1,)), ((), ())),
            preferred_element_type=jnp.float32,
        ) * (channels ** (-0.5))
        at, other = iota((rows, high), 0), iota((rows, high), 1)
        seen = jnp.logical_and((at & 15) == (other & 15), (other >> 4) <= (at >> 4) + c * chunk)
        scores = jnp.where(seen, scores, jnp.float32(-1e30))
        expo = jnp.exp(scores - jnp.max(scores, axis=-1, keepdims=True))
        share = (expo / jnp.sum(expo, axis=-1, keepdims=True)).astype(jnp.bfloat16)
        attended = matmul(share, values[:high]).astype(jnp.bfloat16)
        if c == 0:
            weights[3].wait()
        hidden = (held + matmul(attended, wo[...])).astype(jnp.bfloat16)
        smooth = normalized(hidden.astype(jnp.float32))
        if c == 0:
            weights[4].wait()
        current = matmul(smooth, wt[0])
        lag1[BLOCK + low : BLOCK + high] = matmul(smooth, wt[1])
        lag2[2 * BLOCK + low : 2 * BLOCK + high] = matmul(smooth, wt[2])

        frame = (flat >> 4) + c * chunk
        new_start = jnp.zeros((rows, 1), jnp.int32)
        for t in range(starts.shape[0]):
            new_start = jnp.maximum(new_start, jnp.where(frame >= starts[t], starts[t], 0))
        old_start = jnp.zeros((rows, 1), jnp.int32)
        for t in range(starts.shape[0]):
            old_start = jnp.maximum(old_start, jnp.where(new_start > starts[t], starts[t], 0))
        inside = frame - new_start
        fade = jnp.where(
            jnp.logical_and(new_start > 0, inside < OV),
            (inside + 1).astype(jnp.float32) / float(OV + 1),
            jnp.float32(1.0),
        )

        def mixed(start):
            reach = jnp.broadcast_to(frame - start, (rows, channels))
            one = jnp.where(reach >= 1, lag1[low:high], lag1[BLOCK + low : BLOCK + high])
            two = jnp.where(
                reach >= 2,
                lag2[low:high],
                jnp.where(
                    reach >= 1,
                    lag2[BLOCK + low : BLOCK + high],
                    lag2[2 * BLOCK + low : 2 * BLOCK + high],
                ),
            )
            return current + one + two

        blended = (
            fade * silu(mixed(new_start)) + (1.0 - fade) * silu(mixed(old_start))
        ).astype(jnp.bfloat16)
        turned = matmul(by_position, jnp.concatenate([blended, hidden], axis=1)).astype(jnp.bfloat16)
        ext[c, 1 : BS + 1, 1 : BS + 1] = turned[:, :channels].reshape(BS, BS, chunk, channels)
        kept[c] = turned[:, channels:]

    def span(step, sending):
        if step == 0:
            return pl.ds(1, BS)
        if sending:
            return pl.ds(1 if step < 0 else BS, 1)
        return pl.ds(BS + 1 if step < 0 else 0, 1)

    halos = []
    for c in range(CHUNKS):
        halo = []
        for i, (down, right) in enumerate(
            ((-1, 0), (1, 0), (0, -1), (0, 1), (-1, -1), (-1, 1), (1, -1), (1, 1))
        ):
            to_row, to_column = row + down, column + right
            there = jnp.logical_and(
                jnp.logical_and(to_row >= 0, to_row < PH // BS),
                jnp.logical_and(to_column >= 0, to_column < PW // BS),
            )
            from_row, from_column = row - down, column - right
            comes = jnp.logical_and(
                jnp.logical_and(from_row >= 0, from_row < PH // BS),
                jnp.logical_and(from_column >= 0, from_column < PW // BS),
            )
            peer = device_at((to_row + PH // BS) % (PH // BS), (to_column + PW // BS) % (PW // BS))
            copy = pltpu.make_async_remote_copy(
                src_ref=ext.at[c, span(down, True), span(right, True)],
                dst_ref=ext.at[c, span(down, False), span(right, False)],
                send_sem=halo_sent.at[c, i],
                recv_sem=halo_got.at[c, i],
                device_id={"tm": peer},
                device_id_type=mesh_id,
            )
            halo.append((copy, there, comes))
        halos.append(halo)

    def send_halo(c):
        for copy, there, comes in halos[c]:

            @pl.when(there)
            def _():
                copy.start()

    def back_copy(source, target):
        return pltpu.make_async_remote_copy(
            src_ref=back.at[target],
            dst_ref=returned.at[source],
            send_sem=back_sent.at[target],
            recv_sem=back_got.at[source],
            device_id={"tm": target},
            device_id_type=mesh_id,
        )

    own = pltpu.make_async_copy(back.at[me], returned.at[me], own_sem)

    def convolve(c):
        if c == 0:
            weights[5].wait()
        total = kept[c].astype(jnp.float32) + matmul(
            ext[c, 1 : BS + 1, 1 : BS + 1].reshape(rows, channels), ws[1, 1]
        )
        for copy, there, comes in halos[c]:

            @pl.when(comes)
            def _():
                copy.wait_recv()

        for a in range(3):
            for b in range(3):
                if a != 1 or b != 1:
                    window = ext[c, a : a + BS, b : b + BS].reshape(rows, channels)
                    total = total + matmul(window, ws[a, b])
        back[c * chunk : (c + 1) * chunk] = (
            matmul(by_frame, total.astype(jnp.bfloat16))
            .astype(jnp.bfloat16)
            .reshape(chunk, BLOCK, channels)
        )
        for i in range(chunk):
            target = c * chunk + (local + i) % chunk
            if i == 0:

                @pl.when(target != me)
                def _():
                    back_copy(me, target).start()

                @pl.when(target == me)
                def _():
                    own.start()
            else:
                back_copy(me, target).start()

    for c in range(CHUNKS):
        wait_plane(c)
        blend(c)
        send_halo(c)
        if c >= 1:
            convolve(c - 1)
    convolve(CHUNKS - 1)

    @pl.loop(1, n)
    def _(k):
        in_copy(me, (me + k) % n).wait_send()

    for halo in halos:
        for copy, there, comes in halo:

            @pl.when(there)
            def _():
                copy.wait_send()

    own.wait()

    @pl.loop(1, n)
    def _(k):
        back_copy((me + k) % n, me).wait_recv()

    @pl.loop(1, n)
    def _(k):
        back_copy(me, (me + k) % n).wait_send()


def window_kernel(blocks, out):
    n, block, channels = blocks.shape
    to_window = one_hot(block_position(), n * block)
    out[0] = matmul(to_window, blocks[...].reshape(n * block, channels)).astype(jnp.bfloat16)


def block_body(latents, w_query, w_key, w_value, w_out, w_time, w_space, tile_starts):
    n = lax.axis_size("tm")
    channels = latents.shape[-1]
    chunk = n // CHUNKS
    rows = chunk * BLOCK
    vmem = pl.BlockSpec(memory_space=pltpu.VMEM)
    anywhere = pl.BlockSpec(memory_space=pltpu.HBM)
    dma = pltpu.SemaphoreType.DMA
    bf16 = jnp.bfloat16
    blocks = pl.pallas_call(
        functools.partial(block_kernel, n=n),
        out_shape=jax.ShapeDtypeStruct((n, BLOCK, channels), bf16),
        in_specs=[pl.BlockSpec(memory_space=pltpu.SMEM)] + [anywhere] * 7,
        out_specs=anywhere,
        scratch_shapes=[
            pltpu.VMEM(latents.shape[1:], bf16),
            pltpu.VMEM((channels, 3 * channels), bf16),
            pltpu.VMEM(w_out.shape, bf16),
            pltpu.VMEM(w_time.shape, bf16),
            pltpu.VMEM(w_space.shape, bf16),
            pltpu.VMEM((n, BLOCK, channels), bf16),
            pltpu.VMEM((n, BLOCK, channels), bf16),
            pltpu.VMEM((n * BLOCK, channels), bf16),
            pltpu.VMEM((n * BLOCK, channels), bf16),
            pltpu.VMEM(((n + 1) * BLOCK, channels), jnp.float32),
            pltpu.VMEM(((n + 2) * BLOCK, channels), jnp.float32),
            pltpu.VMEM((CHUNKS, BS + 2, BS + 2, chunk, channels), bf16),
            pltpu.VMEM((CHUNKS, rows, channels), bf16),
            pltpu.VMEM((n, BLOCK, channels), bf16),
            dma((7,)),
            dma((n,)),
            dma((n,)),
            dma((CHUNKS, 8)),
            dma((CHUNKS, 8)),
            dma((n,)),
            dma((n,)),
            dma(()),
        ],
        compiler_params=pltpu.CompilerParams(
            collective_id=0, has_side_effects=True, vmem_limit_bytes=60 * 2**20
        ),
    )(tile_starts, latents, w_query, w_key, w_value, w_out, w_time, w_space)
    return pl.pallas_call(
        window_kernel,
        out_shape=jax.ShapeDtypeStruct(latents.shape, bf16),
        in_specs=[vmem],
        out_specs=vmem,
    )(blocks)


def any_body(latents, *rest):
    frames_dev, row_count, channels = latents.shape
    blocks = (PH // BS) * (PW // BS)
    if frames_dev == 1 and lax.axis_size("tm") == blocks and row_count == PH * PW:
        return block_body(latents, *rest)
    return body(latents, *rest)


def solution(mesh):
    placed = (P(("groups", "tm"), None, None), P(), P(), P(), P(), P(), P(), P("groups"))
    return jax.shard_map(
        any_body, mesh=mesh, in_specs=placed, out_specs=P(("groups", "tm"), None, None), check_vma=False
    )
```

```python
import functools

import jax
import jax.numpy as jnp
from jax import lax
from jax.experimental import pallas as pl
from jax.experimental.pallas import tpu as pltpu
from jax.sharding import PartitionSpec as P

PH = 16
PW = 32
OV = 2


epsilon = 1e-06


def passed_along(block, axis, distance):
    devices = range(lax.axis_size(axis))
    route = [(i - distance, i) for i in devices if i - distance in devices]
    return lax.ppermute(block, axis, route)


def rms_norm(array):
    wide = array.astype(jnp.float32)
    return (wide * lax.rsqrt(jnp.mean(wide * wide, axis=-1, keepdims=True) + epsilon)).astype(
        jnp.bfloat16
    )


def project(array, weight):
    extent = array.shape
    product = jnp.dot(array.reshape(-1, extent[-1]), weight, preferred_element_type=jnp.float32)
    return product.reshape(extent[:-1] + (weight.shape[-1],))


def tile_frames(frames, starts):
    reached = starts[None, :] <= frames[:, None]
    new_start = jnp.max(jnp.where(reached, starts[None, :], 0), axis=1)
    earlier = starts[None, :] < new_start[:, None]
    old_start = jnp.max(jnp.where(earlier, starts[None, :], 0), axis=1)
    inside = frames - new_start
    shared = jnp.logical_and(new_start > 0, inside < OV)
    fade = jnp.where(shared, (inside + 1).astype(jnp.float32) / float(OV + 1), jnp.float32(1.0))
    return (new_start, old_start, fade[:, None, None])


def attend(triple):
    queries, key_rows, values = triple
    length = queries.shape[0]
    scale = queries.shape[-1] ** (-0.5)
    scores = (
        jnp.einsum("fipc,gipc->ipfg", queries, key_rows, preferred_element_type=jnp.float32) * scale
    )
    order = jnp.arange(length)
    causal = order[:, None] >= order[None, :]
    scores = jnp.where(causal[None, None], scores, jnp.float32(-1e30))
    peak = jnp.max(scores, axis=-1, keepdims=True)
    expo = jnp.exp(scores - peak)
    weights = (expo / jnp.sum(expo, axis=-1, keepdims=True)).astype(jnp.bfloat16)
    return jnp.einsum(
        "ipfg,gipc->fipc", weights, values, preferred_element_type=jnp.float32
    ).astype(jnp.bfloat16)


def time_blend(padded, frames, starts, w_time):
    length = frames.shape[0]
    extent = padded.shape
    channels = extent[-1]
    flattened = padded.reshape(-1, channels)
    products = [
        jnp.dot(flattened, w_time[lag_index], preferred_element_type=jnp.float32).reshape(
            extent[0], -1, channels
        )
        for lag_index in range(3)
    ]
    new_start, old_start, fade = tile_frames(frames, starts)

    def mixed(context):
        summed = jnp.zeros((length,) + products[0].shape[1:], jnp.float32)
        for lag_index in range(3):
            actual = jnp.minimum(lag_index, frames - context)
            for delta_back in range(lag_index + 1):
                chosen = (actual == delta_back).astype(jnp.float32)[:, None, None]
                summed = (
                    summed + chosen * products[lag_index][2 - delta_back : 2 - delta_back + length]
                )
        return summed

    blended = fade * jax.nn.silu(mixed(new_start)) + (1.0 - fade) * jax.nn.silu(mixed(old_start))
    return blended.astype(jnp.bfloat16)


def space_mix(blended, hidden, w_space):
    length = blended.shape[0]
    channels = blended.shape[-1]
    spatial = blended.reshape(length, PH, PW, channels)
    padded = jnp.pad(spatial, ((0, 0), (1, 1), (1, 1), (0, 0)))
    summed = hidden.reshape(-1, channels).astype(jnp.float32)
    for row_shift in range(3):
        for col_shift in range(3):
            window = padded[:, row_shift : row_shift + PH, col_shift : col_shift + PW].reshape(
                -1, channels
            )
            summed = summed + jnp.dot(
                window, w_space[row_shift, col_shift], preferred_element_type=jnp.float32
            )
    return summed.reshape(length, PH * PW, channels).astype(jnp.bfloat16)


def body(latents, w_query, w_key, w_value, w_out, w_time, w_space, tile_starts):
    frames_dev, row_count, channels = latents.shape
    devices_tm = lax.axis_size("tm")
    share = row_count // devices_tm
    normed = rms_norm(latents).reshape(frames_dev, devices_tm, share, channels)
    queries = project(normed, w_query).astype(jnp.bfloat16)
    key_rows = project(normed, w_key).astype(jnp.bfloat16)
    values = project(normed, w_value).astype(jnp.bfloat16)
    attended = attend(
        (
            lax.all_to_all(queries, "tm", split_axis=1, concat_axis=0, tiled=True),
            lax.all_to_all(key_rows, "tm", split_axis=1, concat_axis=0, tiled=True),
            lax.all_to_all(values, "tm", split_axis=1, concat_axis=0, tiled=True),
        )
    )
    attended = lax.all_to_all(attended, "tm", split_axis=0, concat_axis=1, tiled=True).reshape(
        frames_dev, row_count, channels
    )
    hidden = (latents.astype(jnp.float32) + project(attended, w_out)).astype(jnp.bfloat16)
    smooth = rms_norm(hidden)
    reach = (frames_dev + 1) // frames_dev
    pieces = [passed_along(smooth, "tm", stride) for stride in range(reach, 0, -1)]
    earlier = jnp.concatenate(pieces, axis=0)
    offset = lax.axis_index("tm") * frames_dev
    frames = offset + jnp.arange(frames_dev)
    blended = time_blend(jnp.concatenate([earlier, smooth], axis=0), frames, tile_starts, w_time)
    return space_mix(blended, hidden, w_space)


TALL = 2
WIDE = 8
DOWN = 8
ACROSS = 4


def iota(shape, dim):
    return lax.broadcasted_iota(jnp.int32, shape, dim)


def one_hot(target, columns):
    rows = target.shape[0]
    return (jnp.broadcast_to(target, (rows, columns)) == iota((rows, columns), 1)).astype(
        jnp.float32
    ).astype(jnp.bfloat16)


def matmul(left, right):
    return jnp.dot(left, right, preferred_element_type=jnp.float32)


def place_of(device):
    core, x, y, z = device % 2, (device // 2) % 2, (device // 4) % 2, device // 8
    return 2 * z + (core + z) % 2, 2 * y + (x + y) % 2


def device_at(row, column):
    z, y = row // 2, column // 2
    return z * 8 + y * 4 + ((column + y) % 2) * 2 + (row + z) % 2


def normalized(wide):
    scale = lax.rsqrt(jnp.mean(wide * wide, axis=-1, keepdims=True) + epsilon)
    return (wide * scale).astype(jnp.bfloat16)


def half_silu(v):
    half = 0.5 * v
    return half + half * jnp.tanh(half)


def block_kernel(
    starts,
    latents,
    wq_any,
    wk_any,
    wv_any,
    wo_any,
    wt_any,
    ws_any,
    returned,
    wqkv,
    wo,
    wt,
    ws,
    arrived,
    bias,
    shifts,
    ext,
    kept,
    sums,
    back,
    weight_sem,
    sent,
    got,
    side_sent,
    side_got,
    rim_sent,
    rim_got,
    back_sent,
    back_got,
    own_sem,
    *,
    n,
):
    channels = latents.shape[-1]
    rows = n * WIDE
    me = lax.axis_index("tm")
    mesh_id = pl.DeviceIdType.MESH

    barrier = pltpu.get_barrier_semaphore()

    @pl.loop(1, n)
    def _(k):
        pl.semaphore_signal(
            barrier, inc=1, device_id={"tm": (me + k) % n}, device_id_type=mesh_id
        )

    row, column = place_of(me)
    owns_in = [
        pltpu.make_async_copy(
            latents.at[row * TALL + g, column], arrived.at[g, me], own_sem.at[0, g]
        )
        for g in range(TALL)
    ]
    for copy in owns_in:
        copy.start()
    weights = [
        pltpu.make_async_copy(source, target, weight_sem.at[i])
        for i, (source, target) in enumerate(
            (
                (wq_any, wqkv.at[:, :channels]),
                (wk_any, wqkv.at[:, channels : 2 * channels]),
                (wv_any, wqkv.at[:, 2 * channels :]),
                (wo_any, wo),
                (wt_any.at[0], wt.at[:, :channels]),
                (wt_any.at[1], wt.at[:, channels : 2 * channels]),
                (wt_any.at[2], wt.at[:, 2 * channels :]),
                (ws_any, ws),
            )
        )
    ]
    for copy in weights:
        copy.start()
    pl.semaphore_wait(barrier, n - 1)

    def in_copy(g, k):
        peer = (me + k * 31) % n
        to_row, to_column = place_of(peer)
        return pltpu.make_async_remote_copy(
            src_ref=latents.at[to_row * TALL + g, to_column],
            dst_ref=arrived.at[g, me],
            send_sem=sent.at[g],
            recv_sem=got.at[g],
            device_id={"tm": peer},
            device_id_type=mesh_id,
        )

    def in_all(g):
        return pltpu.make_async_remote_copy(
            src_ref=arrived.at[g, 1:],
            dst_ref=arrived.at[g, 1:],
            send_sem=sent.at[g],
            recv_sem=got.at[g],
            device_id={"tm": (me + 1) % n},
            device_id_type=mesh_id,
        )

    for g in range(TALL):

        @pl.loop(1, n)
        def _(k):
            in_copy(g, k).start()

    edge = jnp.zeros((n, channels), jnp.bfloat16)

    @pl.when(row == 0)
    def _():
        for i in range(WIDE + 2):
            ext[0, i] = edge

    @pl.when(row == DOWN - 1)
    def _():
        for i in range(WIDE + 2):
            ext[TALL + 1, i] = edge

    @pl.when(column == 0)
    def _():
        for i in range(TALL + 2):
            ext[i, 0] = edge

    @pl.when(column == ACROSS - 1)
    def _():
        for i in range(TALL + 2):
            ext[i, WIDE + 1] = edge

    flat = iota((rows, 1), 0)
    by_position = one_hot((flat % n) * WIDE + flat // n, rows)
    by_frame = one_hot((flat % WIDE) * n + flat // WIDE, rows)

    at, other = iota(bias.shape, 0), iota(bias.shape, 1)
    seen = jnp.logical_and((at & (WIDE - 1)) == (other & (WIDE - 1)), other <= at)
    bias[...] = jnp.where(seen, 0.0, -1e30)

    lanes = shifts.shape[-1]
    frame = iota((rows, lanes), 0) // WIDE
    new_start = jnp.zeros(frame.shape, jnp.int32)
    for t in range(starts.shape[0]):
        new_start = jnp.maximum(new_start, jnp.where(frame >= starts[t], starts[t], 0))
    old_start = jnp.zeros(frame.shape, jnp.int32)
    for t in range(starts.shape[0]):
        old_start = jnp.maximum(old_start, jnp.where(new_start > starts[t], starts[t], 0))
    inside = frame - new_start
    shifts[0] = inside.astype(jnp.float32)
    shifts[1] = (frame - old_start).astype(jnp.float32)
    shifts[2] = jnp.where(
        jnp.logical_and(new_start > 0, inside < OV),
        (inside + 1).astype(jnp.float32) / float(OV + 1),
        jnp.float32(1.0),
    )

    def wide(tile):
        return jnp.concatenate([tile] * (channels // lanes), axis=1)

    def blend(g):
        held = arrived[g].reshape(rows, channels).astype(jnp.float32)
        projected = matmul(normalized(held), wqkv[...]).astype(jnp.bfloat16)
        queries = projected[:, :channels]
        keys = projected[:, channels : 2 * channels]
        values = projected[:, 2 * channels :]
        attended = []
        for low in range(0, rows, rows // PARTS):
            high = low + rows // PARTS
            scores = lax.dot_general(
                queries[low:high],
                keys[:high],
                (((1,), (1,)), ((), ())),
                preferred_element_type=jnp.float32,
            )
            scores = scores * (channels ** (-0.5) * 1.4426950408889634) + bias[low:high, :high]
            expo = jnp.exp2(scores - jnp.max(scores, axis=-1, keepdims=True))
            share = (expo * (1.0 / jnp.sum(expo, axis=-1, keepdims=True))).astype(jnp.bfloat16)
            attended.append(matmul(share, values[:high]).astype(jnp.bfloat16))
        attended = jnp.concatenate(attended, axis=0)
        hidden = (held + matmul(attended, wo[...])).astype(jnp.bfloat16)
        smooth = normalized(hidden.astype(jnp.float32))
        products = matmul(smooth, wt[...])
        current = products[:, :channels]
        none = jnp.zeros((2 * WIDE, channels), jnp.float32)
        lag1 = products[:, channels : 2 * channels]
        lag2 = products[:, 2 * channels :]
        one_back = jnp.concatenate([none[:WIDE], lag1[: rows - WIDE]], axis=0)
        two_one = jnp.concatenate([none[:WIDE], lag2[: rows - WIDE]], axis=0)
        two_back = jnp.concatenate([none, lag2[: rows - 2 * WIDE]], axis=0)

        def mixed(reach):
            one = jnp.where(reach >= 1.0, one_back, lag1)
            two = jnp.where(reach >= 2.0, two_back, jnp.where(reach >= 1.0, two_one, lag2))
            return half_silu(current + one + two)

        fade = wide(shifts[2])
        blended = fade * mixed(wide(shifts[0])) + (1.0 - fade) * mixed(wide(shifts[1]))
        turned = matmul(
            by_position, jnp.concatenate([blended.astype(jnp.bfloat16), hidden], axis=1)
        ).astype(jnp.bfloat16)
        ext[g + 1, 1 : WIDE + 1] = turned[:, :channels].reshape(WIDE, n, channels)
        kept[g] = turned[:, channels:]

    def link(down, right, source, target, send_sem, recv_sem):
        to_row, to_column = row + down, column + right
        there = jnp.logical_and(
            jnp.logical_and(to_row >= 0, to_row < DOWN),
            jnp.logical_and(to_column >= 0, to_column < ACROSS),
        )
        from_row, from_column = row - down, column - right
        comes = jnp.logical_and(
            jnp.logical_and(from_row >= 0, from_row < DOWN),
            jnp.logical_and(from_column >= 0, from_column < ACROSS),
        )
        peer = device_at((to_row + DOWN) % DOWN, (to_column + ACROSS) % ACROSS)
        copy = pltpu.make_async_remote_copy(
            src_ref=source,
            dst_ref=target,
            send_sem=send_sem,
            recv_sem=recv_sem,
            device_id={"tm": peer},
            device_id_type=mesh_id,
        )
        return copy, there, comes

    sides = [
        [
            link(0, -1, ext.at[e, 1], ext.at[e, WIDE + 1], side_sent.at[e, 0], side_got.at[e, 0]),
            link(0, 1, ext.at[e, WIDE], ext.at[e, 0], side_sent.at[e, 1], side_got.at[e, 1]),
        ]
        for e in range(1, TALL + 1)
    ]
    inner = pl.ds(1, WIDE)
    rims = [
        [
            link(d, -1, ext.at[e, 1], ext.at[t, WIDE + 1], rim_sent.at[i, 1], rim_got.at[i, 1]),
            link(d, 1, ext.at[e, WIDE], ext.at[t, 0], rim_sent.at[i, 2], rim_got.at[i, 2]),
            link(d, 0, ext.at[e, inner], ext.at[t, inner], rim_sent.at[i, 0], rim_got.at[i, 0]),
        ]
        for i, (d, e, t) in enumerate(((-1, 1, TALL + 1), (1, TALL, 0)))
    ]

    def send(links):
        for copy, there, comes in links:

            @pl.when(there)
            def _():
                copy.start()

    def receive(links):
        for copy, there, comes in links:

            @pl.when(comes)
            def _():
                copy.wait_recv()

    def taps(g, e, columns):
        return sum(
            matmul(ext[e, b : b + WIDE].reshape(rows, channels), ws[e - g, b]) for b in columns
        )

    def back_copy(g, k):
        peer = (me + k) % n
        return pltpu.make_async_remote_copy(
            src_ref=back.at[g, peer],
            dst_ref=returned.at[row * TALL + g, column],
            send_sem=back_sent,
            recv_sem=back_got,
            device_id={"tm": peer},
            device_id_type=mesh_id,
        )

    owns_out = [
        pltpu.make_async_copy(
            back.at[g, me], returned.at[row * TALL + g, column], own_sem.at[1, g]
        )
        for g in range(TALL)
    ]

    def finish(g, total):
        total = (kept[g].astype(jnp.float32) + total).astype(jnp.bfloat16)
        back[g] = matmul(by_frame, total).astype(jnp.bfloat16).reshape(n, WIDE, channels)

        @pl.loop(1, n)
        def _(k):
            back_copy(g, k).start()

        owns_out[g].start()

    for copy in weights:
        copy.wait()
    for copy in owns_in:
        copy.wait()

    in_all(0).wait_recv()
    blend(0)
    send(sides[0])
    send(rims[0])
    sums[0] = taps(0, 1, (1,))
    sums[1] = taps(1, 1, (1,))

    in_all(1).wait_recv()
    blend(1)
    send(sides[1])
    send(rims[1])
    sums[1] = sums[1] + taps(1, 2, (1,))
    receive(sides[0])
    receive(rims[0])
    sums[1] = sums[1] + taps(1, 1, (0, 2)) + taps(1, 3, (0, 1, 2))
    receive(sides[1])
    finish(1, sums[1] + taps(1, 2, (0, 2)))
    sums[0] = sums[0] + taps(0, 1, (0, 2)) + taps(0, 2, (0, 1, 2))
    receive(rims[1])
    finish(0, sums[0] + taps(0, 0, (0, 1, 2)))

    for g in range(TALL):
        in_all(g).wait_send()

    for links in sides + rims:
        for copy, there, comes in links:

            @pl.when(there)
            def _():
                copy.wait_send()

    for own in owns_out:
        own.wait()
    everything = pltpu.make_async_remote_copy(
        src_ref=back.at[:, 1:],
        dst_ref=back.at[:, 1:],
        send_sem=back_sent,
        recv_sem=back_got,
        device_id={"tm": (me + 1) % n},
        device_id_type=mesh_id,
    )
    everything.wait_send()
    everything.wait_recv()


PARTS = 2


def settle_kernel(source, target):
    target[...] = source[...]


def block_body(latents, w_query, w_key, w_value, w_out, w_time, w_space, tile_starts):
    n = lax.axis_size("tm")
    channels = latents.shape[-1]
    rows = n * WIDE
    vmem = pl.BlockSpec(memory_space=pltpu.VMEM)
    anywhere = pl.BlockSpec(memory_space=pltpu.HBM)
    dma = pltpu.SemaphoreType.DMA
    bf16 = jnp.bfloat16
    spaced = (PH, PW // WIDE, WIDE, channels)
    blocks = pl.pallas_call(
        functools.partial(block_kernel, n=n),
        out_shape=jax.ShapeDtypeStruct(spaced, bf16),
        in_specs=[pl.BlockSpec(memory_space=pltpu.SMEM)] + [anywhere] * 7,
        out_specs=anywhere,
        scratch_shapes=[
            pltpu.VMEM((channels, 3 * channels), bf16),
            pltpu.VMEM(w_out.shape, bf16),
            pltpu.VMEM((channels, 3 * channels), bf16),
            pltpu.VMEM(w_space.shape, bf16),
            pltpu.VMEM((TALL, n, WIDE, channels), bf16),
            pltpu.VMEM((rows, rows), jnp.float32),
            pltpu.VMEM((3, rows, 128), jnp.float32),
            pltpu.VMEM((TALL + 2, WIDE + 2, n, channels), bf16),
            pltpu.VMEM((TALL, rows, channels), bf16),
            pltpu.VMEM((TALL, rows, channels), jnp.float32),
            pltpu.VMEM((TALL, n, WIDE, channels), bf16),
            dma((8,)),
            dma((TALL,)),
            dma((TALL,)),
            dma((TALL + 1, 2)),
            dma((TALL + 1, 2)),
            dma((2, 3)),
            dma((2, 3)),
            dma(()),
            dma(()),
            dma((2, TALL)),
        ],
        compiler_params=pltpu.CompilerParams(
            collective_id=0, has_side_effects=True, vmem_limit_bytes=60 * 2**20
        ),
    )(tile_starts, latents.reshape(spaced), w_query, w_key, w_value, w_out, w_time, w_space)
    settled = pl.pallas_call(
        settle_kernel,
        out_shape=jax.ShapeDtypeStruct(spaced, bf16),
        in_specs=[vmem],
        out_specs=vmem,
    )(blocks)
    return settled.reshape(latents.shape)


def any_body(latents, *rest):
    frames_dev, row_count, channels = latents.shape
    fits = row_count == PH * PW and PH == TALL * DOWN and PW == WIDE * ACROSS
    if frames_dev == 1 and lax.axis_size("tm") == DOWN * ACROSS and fits:
        return block_body(latents, *rest)
    return body(latents, *rest)


def solution(mesh):
    placed = (P(("groups", "tm"), None, None), P(), P(), P(), P(), P(), P(), P("groups"))
    return jax.shard_map(
        any_body, mesh=mesh, in_specs=placed, out_specs=P(("groups", "tm"), None, None), check_vma=False
    )
```

```python
import functools

import jax
import jax.numpy as jnp
from jax import lax
from jax.experimental import pallas as pl
from jax.experimental.pallas import tpu as pltpu
from jax.sharding import PartitionSpec as P

PH = 16
PW = 32
OV = 2


epsilon = 1e-06


def passed_along(block, axis, distance):
    devices = range(lax.axis_size(axis))
    route = [(i - distance, i) for i in devices if i - distance in devices]
    return lax.ppermute(block, axis, route)


def rms_norm(array):
    wide = array.astype(jnp.float32)
    return (wide * lax.rsqrt(jnp.mean(wide * wide, axis=-1, keepdims=True) + epsilon)).astype(
        jnp.bfloat16
    )


def project(array, weight):
    extent = array.shape
    product = jnp.dot(array.reshape(-1, extent[-1]), weight, preferred_element_type=jnp.float32)
    return product.reshape(extent[:-1] + (weight.shape[-1],))


def tile_frames(frames, starts):
    reached = starts[None, :] <= frames[:, None]
    new_start = jnp.max(jnp.where(reached, starts[None, :], 0), axis=1)
    earlier = starts[None, :] < new_start[:, None]
    old_start = jnp.max(jnp.where(earlier, starts[None, :], 0), axis=1)
    inside = frames - new_start
    shared = jnp.logical_and(new_start > 0, inside < OV)
    fade = jnp.where(shared, (inside + 1).astype(jnp.float32) / float(OV + 1), jnp.float32(1.0))
    return (new_start, old_start, fade[:, None, None])


def attend(triple):
    queries, key_rows, values = triple
    length = queries.shape[0]
    scale = queries.shape[-1] ** (-0.5)
    scores = (
        jnp.einsum("fipc,gipc->ipfg", queries, key_rows, preferred_element_type=jnp.float32) * scale
    )
    order = jnp.arange(length)
    causal = order[:, None] >= order[None, :]
    scores = jnp.where(causal[None, None], scores, jnp.float32(-1e30))
    peak = jnp.max(scores, axis=-1, keepdims=True)
    expo = jnp.exp(scores - peak)
    weights = (expo / jnp.sum(expo, axis=-1, keepdims=True)).astype(jnp.bfloat16)
    return jnp.einsum(
        "ipfg,gipc->fipc", weights, values, preferred_element_type=jnp.float32
    ).astype(jnp.bfloat16)


def time_blend(padded, frames, starts, w_time):
    length = frames.shape[0]
    extent = padded.shape
    channels = extent[-1]
    flattened = padded.reshape(-1, channels)
    products = [
        jnp.dot(flattened, w_time[lag_index], preferred_element_type=jnp.float32).reshape(
            extent[0], -1, channels
        )
        for lag_index in range(3)
    ]
    new_start, old_start, fade = tile_frames(frames, starts)

    def mixed(context):
        summed = jnp.zeros((length,) + products[0].shape[1:], jnp.float32)
        for lag_index in range(3):
            actual = jnp.minimum(lag_index, frames - context)
            for delta_back in range(lag_index + 1):
                chosen = (actual == delta_back).astype(jnp.float32)[:, None, None]
                summed = (
                    summed + chosen * products[lag_index][2 - delta_back : 2 - delta_back + length]
                )
        return summed

    blended = fade * jax.nn.silu(mixed(new_start)) + (1.0 - fade) * jax.nn.silu(mixed(old_start))
    return blended.astype(jnp.bfloat16)


def space_mix(blended, hidden, w_space):
    length = blended.shape[0]
    channels = blended.shape[-1]
    spatial = blended.reshape(length, PH, PW, channels)
    padded = jnp.pad(spatial, ((0, 0), (1, 1), (1, 1), (0, 0)))
    summed = hidden.reshape(-1, channels).astype(jnp.float32)
    for row_shift in range(3):
        for col_shift in range(3):
            window = padded[:, row_shift : row_shift + PH, col_shift : col_shift + PW].reshape(
                -1, channels
            )
            summed = summed + jnp.dot(
                window, w_space[row_shift, col_shift], preferred_element_type=jnp.float32
            )
    return summed.reshape(length, PH * PW, channels).astype(jnp.bfloat16)


def body(latents, w_query, w_key, w_value, w_out, w_time, w_space, tile_starts):
    frames_dev, row_count, channels = latents.shape
    devices_tm = lax.axis_size("tm")
    share = row_count // devices_tm
    normed = rms_norm(latents).reshape(frames_dev, devices_tm, share, channels)
    queries = project(normed, w_query).astype(jnp.bfloat16)
    key_rows = project(normed, w_key).astype(jnp.bfloat16)
    values = project(normed, w_value).astype(jnp.bfloat16)
    attended = attend(
        (
            lax.all_to_all(queries, "tm", split_axis=1, concat_axis=0, tiled=True),
            lax.all_to_all(key_rows, "tm", split_axis=1, concat_axis=0, tiled=True),
            lax.all_to_all(values, "tm", split_axis=1, concat_axis=0, tiled=True),
        )
    )
    attended = lax.all_to_all(attended, "tm", split_axis=0, concat_axis=1, tiled=True).reshape(
        frames_dev, row_count, channels
    )
    hidden = (latents.astype(jnp.float32) + project(attended, w_out)).astype(jnp.bfloat16)
    smooth = rms_norm(hidden)
    reach = (frames_dev + 1) // frames_dev
    pieces = [passed_along(smooth, "tm", stride) for stride in range(reach, 0, -1)]
    earlier = jnp.concatenate(pieces, axis=0)
    offset = lax.axis_index("tm") * frames_dev
    frames = offset + jnp.arange(frames_dev)
    blended = time_blend(jnp.concatenate([earlier, smooth], axis=0), frames, tile_starts, w_time)
    return space_mix(blended, hidden, w_space)


TALL = 2
WIDE = 8
DOWN = 8
ACROSS = 4


def iota(shape, dim):
    return lax.broadcasted_iota(jnp.int32, shape, dim)


def one_hot(target, columns):
    rows = target.shape[0]
    return (jnp.broadcast_to(target, (rows, columns)) == iota((rows, columns), 1)).astype(
        jnp.float32
    ).astype(jnp.bfloat16)


def matmul(left, right):
    return jnp.dot(left, right, preferred_element_type=jnp.float32)


def place_of(device):
    core, x, y, z = device % 2, (device // 2) % 2, (device // 4) % 2, device // 8
    return 2 * z + (core + z) % 2, 2 * y + (x + y) % 2


def device_at(row, column):
    z, y = row // 2, column // 2
    return z * 8 + y * 4 + ((column + y) % 2) * 2 + (row + z) % 2


def normalized(wide):
    scale = lax.rsqrt(jnp.mean(wide * wide, axis=-1, keepdims=True) + epsilon)
    return (wide * scale).astype(jnp.bfloat16)


def half_silu(v):
    half = 0.5 * v
    return half + half * jnp.tanh(half)


def block_kernel(
    starts,
    latents,
    wq_any,
    wk_any,
    wv_any,
    wo_any,
    wt_any,
    ws_any,
    returned,
    wqkv,
    wo,
    wt,
    ws,
    arrived,
    bias,
    shifts,
    ext,
    kept,
    sums,
    back,
    weight_sem,
    sent,
    got,
    side_sent,
    side_got,
    rim_sent,
    rim_got,
    back_sent,
    back_got,
    own_sem,
    *,
    n,
):
    channels = latents.shape[-1]
    rows = n * WIDE
    me = lax.axis_index("tm")
    mesh_id = pl.DeviceIdType.MESH

    barrier = pltpu.get_barrier_semaphore()

    @pl.loop(1, n)
    def _(k):
        pl.semaphore_signal(
            barrier, inc=1, device_id={"tm": (me + k) % n}, device_id_type=mesh_id
        )

    row, column = place_of(me)
    owns_in = [
        pltpu.make_async_copy(
            latents.at[row * TALL + g, column], arrived.at[g, me], own_sem.at[0, g]
        )
        for g in range(TALL)
    ]
    for copy in owns_in:
        copy.start()
    weights = [
        pltpu.make_async_copy(source, target, weight_sem.at[i])
        for i, (source, target) in enumerate(
            (
                (wq_any, wqkv.at[:, :channels]),
                (wk_any, wqkv.at[:, channels : 2 * channels]),
                (wv_any, wqkv.at[:, 2 * channels :]),
                (wo_any, wo),
                (wt_any.at[0], wt.at[:, :channels]),
                (wt_any.at[1], wt.at[:, channels : 2 * channels]),
                (wt_any.at[2], wt.at[:, 2 * channels :]),
                (ws_any, ws),
            )
        )
    ]
    for copy in weights:
        copy.start()
    pl.semaphore_wait(barrier, n - 1)

    def in_copy(g, k):
        peer = (me + k * 31) % n
        to_row, to_column = place_of(peer)
        return pltpu.make_async_remote_copy(
            src_ref=latents.at[to_row * TALL + g, to_column],
            dst_ref=arrived.at[g, me],
            send_sem=sent.at[g],
            recv_sem=got.at[g],
            device_id={"tm": peer},
            device_id_type=mesh_id,
        )

    def in_all(g):
        return pltpu.make_async_remote_copy(
            src_ref=arrived.at[g, 1:],
            dst_ref=arrived.at[g, 1:],
            send_sem=sent.at[g],
            recv_sem=got.at[g],
            device_id={"tm": (me + 1) % n},
            device_id_type=mesh_id,
        )

    for g in range(TALL):

        @pl.loop(1, n)
        def _(k):
            in_copy(g, k).start()

    edge = jnp.zeros((n, channels), jnp.bfloat16)

    @pl.when(row == 0)
    def _():
        for i in range(WIDE + 2):
            ext[0, i] = edge

    @pl.when(row == DOWN - 1)
    def _():
        for i in range(WIDE + 2):
            ext[TALL + 1, i] = edge

    @pl.when(column == 0)
    def _():
        for i in range(TALL + 2):
            ext[i, 0] = edge

    @pl.when(column == ACROSS - 1)
    def _():
        for i in range(TALL + 2):
            ext[i, WIDE + 1] = edge

    flat = iota((rows, 1), 0)
    by_position = one_hot((flat % n) * WIDE + flat // n, rows)
    by_frame = one_hot((flat % WIDE) * n + flat // WIDE, rows)

    at, other = iota(bias.shape, 0), iota(bias.shape, 1)
    seen = jnp.logical_and((at & (WIDE - 1)) == (other & (WIDE - 1)), other <= at)
    bias[...] = jnp.where(seen, 0.0, -1e30)

    lanes = shifts.shape[-1]
    frame = iota((rows, lanes), 0) // WIDE
    new_start = jnp.zeros(frame.shape, jnp.int32)
    for t in range(starts.shape[0]):
        new_start = jnp.maximum(new_start, jnp.where(frame >= starts[t], starts[t], 0))
    old_start = jnp.zeros(frame.shape, jnp.int32)
    for t in range(starts.shape[0]):
        old_start = jnp.maximum(old_start, jnp.where(new_start > starts[t], starts[t], 0))
    inside = frame - new_start
    shifts[0] = inside.astype(jnp.float32)
    shifts[1] = (frame - old_start).astype(jnp.float32)
    shifts[2] = jnp.where(
        jnp.logical_and(new_start > 0, inside < OV),
        (inside + 1).astype(jnp.float32) / float(OV + 1),
        jnp.float32(1.0),
    )

    def wide(tile):
        return jnp.concatenate([tile] * (channels // lanes), axis=1)

    def blend(g):
        held = arrived[g].reshape(rows, channels).astype(jnp.float32)
        projected = matmul(normalized(held), wqkv[...]).astype(jnp.bfloat16)
        queries = projected[:, :channels]
        keys = projected[:, channels : 2 * channels]
        values = projected[:, 2 * channels :]
        attended = []
        for low in range(0, rows, rows // PARTS):
            high = low + rows // PARTS
            scores = lax.dot_general(
                queries[low:high],
                keys[:high],
                (((1,), (1,)), ((), ())),
                preferred_element_type=jnp.float32,
            )
            scores = scores * (channels ** (-0.5) * 1.4426950408889634) + bias[low:high, :high]
            expo = jnp.exp2(scores - jnp.max(scores, axis=-1, keepdims=True))
            share = (expo * (1.0 / jnp.sum(expo, axis=-1, keepdims=True))).astype(jnp.bfloat16)
            attended.append(matmul(share, values[:high]).astype(jnp.bfloat16))
        attended = jnp.concatenate(attended, axis=0)
        hidden = (held + matmul(attended, wo[...])).astype(jnp.bfloat16)
        smooth = normalized(hidden.astype(jnp.float32))
        products = matmul(smooth, wt[...])
        current = products[:, :channels]
        none = jnp.zeros((2 * WIDE, channels), jnp.float32)
        lag1 = products[:, channels : 2 * channels]
        lag2 = products[:, 2 * channels :]
        one_back = jnp.concatenate([none[:WIDE], lag1[: rows - WIDE]], axis=0)
        two_one = jnp.concatenate([none[:WIDE], lag2[: rows - WIDE]], axis=0)
        two_back = jnp.concatenate([none, lag2[: rows - 2 * WIDE]], axis=0)

        def mixed(reach):
            one = jnp.where(reach >= 1.0, one_back, lag1)
            two = jnp.where(reach >= 2.0, two_back, jnp.where(reach >= 1.0, two_one, lag2))
            return half_silu(current + one + two)

        fade = wide(shifts[2])
        blended = fade * mixed(wide(shifts[0])) + (1.0 - fade) * mixed(wide(shifts[1]))
        turned = matmul(by_position, blended.astype(jnp.bfloat16)).astype(jnp.bfloat16)
        ext[g + 1, 1 : WIDE + 1] = turned.reshape(WIDE, n, channels)
        return hidden

    def link(down, right, source, target, send_sem, recv_sem):
        to_row, to_column = row + down, column + right
        there = jnp.logical_and(
            jnp.logical_and(to_row >= 0, to_row < DOWN),
            jnp.logical_and(to_column >= 0, to_column < ACROSS),
        )
        from_row, from_column = row - down, column - right
        comes = jnp.logical_and(
            jnp.logical_and(from_row >= 0, from_row < DOWN),
            jnp.logical_and(from_column >= 0, from_column < ACROSS),
        )
        peer = device_at((to_row + DOWN) % DOWN, (to_column + ACROSS) % ACROSS)
        copy = pltpu.make_async_remote_copy(
            src_ref=source,
            dst_ref=target,
            send_sem=send_sem,
            recv_sem=recv_sem,
            device_id={"tm": peer},
            device_id_type=mesh_id,
        )
        return copy, there, comes

    sides = [
        [
            link(0, -1, ext.at[e, 1], ext.at[e, WIDE + 1], side_sent.at[e, 0], side_got.at[e, 0]),
            link(0, 1, ext.at[e, WIDE], ext.at[e, 0], side_sent.at[e, 1], side_got.at[e, 1]),
        ]
        for e in range(1, TALL + 1)
    ]
    inner = pl.ds(1, WIDE)
    rims = [
        [
            link(d, -1, ext.at[e, 1], ext.at[t, WIDE + 1], rim_sent.at[i, 1], rim_got.at[i, 1]),
            link(d, 1, ext.at[e, WIDE], ext.at[t, 0], rim_sent.at[i, 2], rim_got.at[i, 2]),
            link(d, 0, ext.at[e, inner], ext.at[t, inner], rim_sent.at[i, 0], rim_got.at[i, 0]),
        ]
        for i, (d, e, t) in enumerate(((-1, 1, TALL + 1), (1, TALL, 0)))
    ]

    def send(links):
        for copy, there, comes in links:

            @pl.when(there)
            def _():
                copy.start()

    def receive(links):
        for copy, there, comes in links:

            @pl.when(comes)
            def _():
                copy.wait_recv()

    def taps(g, e, columns):
        return sum(
            matmul(ext[e, b : b + WIDE].reshape(rows, channels), ws[e - g, b]) for b in columns
        )

    def back_copy(g, k):
        peer = (me + k) % n
        return pltpu.make_async_remote_copy(
            src_ref=back.at[g, peer],
            dst_ref=returned.at[row * TALL + g, column],
            send_sem=back_sent,
            recv_sem=back_got,
            device_id={"tm": peer},
            device_id_type=mesh_id,
        )

    owns_out = [
        pltpu.make_async_copy(
            back.at[g, me], returned.at[row * TALL + g, column], own_sem.at[1, g]
        )
        for g in range(TALL)
    ]

    def finish(g, total):
        total = (kept[g] + total).astype(jnp.bfloat16)
        back[g] = matmul(by_frame, total).astype(jnp.bfloat16).reshape(n, WIDE, channels)

        @pl.loop(1, n)
        def _(k):
            back_copy(g, k).start()

        owns_out[g].start()

    for copy in weights:
        copy.wait()
    for copy in owns_in:
        copy.wait()

    in_all(0).wait_recv()
    hidden = blend(0)
    send(sides[0])
    send(rims[0])
    kept[0] = matmul(by_position, hidden)
    sums[0] = taps(0, 1, (1,))
    sums[1] = taps(1, 1, (1,))

    in_all(1).wait_recv()
    hidden = blend(1)
    send(sides[1])
    send(rims[1])
    kept[1] = matmul(by_position, hidden)
    sums[1] = sums[1] + taps(1, 2, (1,))
    receive(sides[0])
    receive(rims[0])
    sums[1] = sums[1] + taps(1, 1, (0, 2)) + taps(1, 3, (0, 1, 2))
    receive(sides[1])
    finish(1, sums[1] + taps(1, 2, (0, 2)))
    sums[0] = sums[0] + taps(0, 1, (0, 2)) + taps(0, 2, (0, 1, 2))
    receive(rims[1])
    finish(0, sums[0] + taps(0, 0, (0, 1, 2)))

    for g in range(TALL):
        in_all(g).wait_send()

    for links in sides + rims:
        for copy, there, comes in links:

            @pl.when(there)
            def _():
                copy.wait_send()

    for own in owns_out:
        own.wait()
    everything = pltpu.make_async_remote_copy(
        src_ref=back.at[:, 1:],
        dst_ref=back.at[:, 1:],
        send_sem=back_sent,
        recv_sem=back_got,
        device_id={"tm": (me + 1) % n},
        device_id_type=mesh_id,
    )
    everything.wait_send()
    everything.wait_recv()


PARTS = 1


def settle_kernel(source, target, sem):
    copy = pltpu.make_async_copy(source, target, sem)
    copy.start()
    copy.wait()


def block_body(latents, w_query, w_key, w_value, w_out, w_time, w_space, tile_starts):
    n = lax.axis_size("tm")
    channels = latents.shape[-1]
    rows = n * WIDE
    anywhere = pl.BlockSpec(memory_space=pltpu.HBM)
    dma = pltpu.SemaphoreType.DMA
    bf16 = jnp.bfloat16
    spaced = (PH, PW // WIDE, WIDE, channels)
    blocks = pl.pallas_call(
        functools.partial(block_kernel, n=n),
        out_shape=jax.ShapeDtypeStruct(spaced, bf16),
        in_specs=[pl.BlockSpec(memory_space=pltpu.SMEM)] + [anywhere] * 7,
        out_specs=pl.BlockSpec(memory_space=pl.ANY),
        scratch_shapes=[
            pltpu.VMEM((channels, 3 * channels), bf16),
            pltpu.VMEM(w_out.shape, bf16),
            pltpu.VMEM((channels, 3 * channels), bf16),
            pltpu.VMEM(w_space.shape, bf16),
            pltpu.VMEM((TALL, n, WIDE, channels), bf16),
            pltpu.VMEM((rows, rows), jnp.float32),
            pltpu.VMEM((3, rows, 128), jnp.float32),
            pltpu.VMEM((TALL + 2, WIDE + 2, n, channels), bf16),
            pltpu.VMEM((TALL, rows, channels), jnp.float32),
            pltpu.VMEM((TALL, rows, channels), jnp.float32),
            pltpu.VMEM((TALL, n, WIDE, channels), bf16),
            dma((8,)),
            dma((TALL,)),
            dma((TALL,)),
            dma((TALL + 1, 2)),
            dma((TALL + 1, 2)),
            dma((2, 3)),
            dma((2, 3)),
            dma(()),
            dma(()),
            dma((2, TALL)),
        ],
        compiler_params=pltpu.CompilerParams(
            collective_id=0, has_side_effects=True, vmem_limit_bytes=53 * 2**20
        ),
    )(tile_starts, latents.reshape(spaced), w_query, w_key, w_value, w_out, w_time, w_space)
    settled = pl.pallas_call(
        settle_kernel,
        out_shape=jax.ShapeDtypeStruct(spaced, bf16),
        in_specs=[pl.BlockSpec(memory_space=pl.ANY)],
        out_specs=anywhere,
        scratch_shapes=[dma(())],
        compiler_params=pltpu.CompilerParams(vmem_limit_bytes=2**20),
    )(blocks)
    return settled.reshape(latents.shape)


def any_body(latents, *rest):
    frames_dev, row_count, channels = latents.shape
    fits = row_count == PH * PW and PH == TALL * DOWN and PW == WIDE * ACROSS
    if frames_dev == 1 and lax.axis_size("tm") == DOWN * ACROSS and fits:
        return block_body(latents, *rest)
    return body(latents, *rest)


def solution(mesh):
    placed = (P(("groups", "tm"), None, None), P(), P(), P(), P(), P(), P(), P("groups"))
    return jax.shard_map(
        any_body, mesh=mesh, in_specs=placed, out_specs=P(("groups", "tm"), None, None), check_vma=False
    )
```

```python
import functools

import jax
import jax.numpy as jnp
from jax import lax
from jax.experimental import pallas as pl
from jax.experimental.pallas import tpu as pltpu
from jax.sharding import PartitionSpec as P

PH = 16
PW = 32
OV = 2


epsilon = 1e-06


def passed_along(block, axis, distance):
    devices = range(lax.axis_size(axis))
    route = [(i - distance, i) for i in devices if i - distance in devices]
    return lax.ppermute(block, axis, route)


def rms_norm(array):
    wide = array.astype(jnp.float32)
    return (wide * lax.rsqrt(jnp.mean(wide * wide, axis=-1, keepdims=True) + epsilon)).astype(
        jnp.bfloat16
    )


def project(array, weight):
    extent = array.shape
    product = jnp.dot(array.reshape(-1, extent[-1]), weight, preferred_element_type=jnp.float32)
    return product.reshape(extent[:-1] + (weight.shape[-1],))


def tile_frames(frames, starts):
    reached = starts[None, :] <= frames[:, None]
    new_start = jnp.max(jnp.where(reached, starts[None, :], 0), axis=1)
    earlier = starts[None, :] < new_start[:, None]
    old_start = jnp.max(jnp.where(earlier, starts[None, :], 0), axis=1)
    inside = frames - new_start
    shared = jnp.logical_and(new_start > 0, inside < OV)
    fade = jnp.where(shared, (inside + 1).astype(jnp.float32) / float(OV + 1), jnp.float32(1.0))
    return (new_start, old_start, fade[:, None, None])


def attend(triple):
    queries, key_rows, values = triple
    length = queries.shape[0]
    scale = queries.shape[-1] ** (-0.5)
    scores = (
        jnp.einsum("fipc,gipc->ipfg", queries, key_rows, preferred_element_type=jnp.float32) * scale
    )
    order = jnp.arange(length)
    causal = order[:, None] >= order[None, :]
    scores = jnp.where(causal[None, None], scores, jnp.float32(-1e30))
    peak = jnp.max(scores, axis=-1, keepdims=True)
    expo = jnp.exp(scores - peak)
    weights = (expo / jnp.sum(expo, axis=-1, keepdims=True)).astype(jnp.bfloat16)
    return jnp.einsum(
        "ipfg,gipc->fipc", weights, values, preferred_element_type=jnp.float32
    ).astype(jnp.bfloat16)


def time_blend(padded, frames, starts, w_time):
    length = frames.shape[0]
    extent = padded.shape
    channels = extent[-1]
    flattened = padded.reshape(-1, channels)
    products = [
        jnp.dot(flattened, w_time[lag_index], preferred_element_type=jnp.float32).reshape(
            extent[0], -1, channels
        )
        for lag_index in range(3)
    ]
    new_start, old_start, fade = tile_frames(frames, starts)

    def mixed(context):
        summed = jnp.zeros((length,) + products[0].shape[1:], jnp.float32)
        for lag_index in range(3):
            actual = jnp.minimum(lag_index, frames - context)
            for delta_back in range(lag_index + 1):
                chosen = (actual == delta_back).astype(jnp.float32)[:, None, None]
                summed = (
                    summed + chosen * products[lag_index][2 - delta_back : 2 - delta_back + length]
                )
        return summed

    blended = fade * jax.nn.silu(mixed(new_start)) + (1.0 - fade) * jax.nn.silu(mixed(old_start))
    return blended.astype(jnp.bfloat16)


def space_mix(blended, hidden, w_space):
    length = blended.shape[0]
    channels = blended.shape[-1]
    spatial = blended.reshape(length, PH, PW, channels)
    padded = jnp.pad(spatial, ((0, 0), (1, 1), (1, 1), (0, 0)))
    summed = hidden.reshape(-1, channels).astype(jnp.float32)
    for row_shift in range(3):
        for col_shift in range(3):
            window = padded[:, row_shift : row_shift + PH, col_shift : col_shift + PW].reshape(
                -1, channels
            )
            summed = summed + jnp.dot(
                window, w_space[row_shift, col_shift], preferred_element_type=jnp.float32
            )
    return summed.reshape(length, PH * PW, channels).astype(jnp.bfloat16)


def body(latents, w_query, w_key, w_value, w_out, w_time, w_space, tile_starts):
    frames_dev, row_count, channels = latents.shape
    devices_tm = lax.axis_size("tm")
    share = row_count // devices_tm
    normed = rms_norm(latents).reshape(frames_dev, devices_tm, share, channels)
    queries = project(normed, w_query).astype(jnp.bfloat16)
    key_rows = project(normed, w_key).astype(jnp.bfloat16)
    values = project(normed, w_value).astype(jnp.bfloat16)
    attended = attend(
        (
            lax.all_to_all(queries, "tm", split_axis=1, concat_axis=0, tiled=True),
            lax.all_to_all(key_rows, "tm", split_axis=1, concat_axis=0, tiled=True),
            lax.all_to_all(values, "tm", split_axis=1, concat_axis=0, tiled=True),
        )
    )
    attended = lax.all_to_all(attended, "tm", split_axis=0, concat_axis=1, tiled=True).reshape(
        frames_dev, row_count, channels
    )
    hidden = (latents.astype(jnp.float32) + project(attended, w_out)).astype(jnp.bfloat16)
    smooth = rms_norm(hidden)
    reach = (frames_dev + 1) // frames_dev
    pieces = [passed_along(smooth, "tm", stride) for stride in range(reach, 0, -1)]
    earlier = jnp.concatenate(pieces, axis=0)
    offset = lax.axis_index("tm") * frames_dev
    frames = offset + jnp.arange(frames_dev)
    blended = time_blend(jnp.concatenate([earlier, smooth], axis=0), frames, tile_starts, w_time)
    return space_mix(blended, hidden, w_space)


TALL = 2
WIDE = 8
DOWN = 8
ACROSS = 4


def iota(shape, dim):
    return lax.broadcasted_iota(jnp.int32, shape, dim)


def one_hot(target, columns):
    rows = target.shape[0]
    return (jnp.broadcast_to(target, (rows, columns)) == iota((rows, columns), 1)).astype(
        jnp.float32
    ).astype(jnp.bfloat16)


def matmul(left, right):
    return jnp.dot(left, right, preferred_element_type=jnp.float32)


def place_of(device):
    core, x = lax.rem(device, 2), lax.rem(lax.div(device, 2), 2)
    y, z = lax.rem(lax.div(device, 4), 2), lax.div(device, 8)
    return 2 * z + lax.rem(core + z, 2), 2 * y + lax.rem(x + y, 2)


def device_at(row, column):
    z, y = lax.div(row, 2), lax.div(column, 2)
    return z * 8 + y * 4 + lax.rem(column + y, 2) * 2 + lax.rem(row + z, 2)


def normalized(wide):
    scale = lax.rsqrt(jnp.mean(wide * wide, axis=-1, keepdims=True) + epsilon)
    return (wide * scale).astype(jnp.bfloat16)


def half_silu(v):
    half = 0.5 * v
    return half + half * jnp.tanh(half)


def block_kernel(
    starts,
    latents,
    wq_any,
    wk_any,
    wv_any,
    wo_any,
    wt_any,
    ws_any,
    returned,
    wqkv,
    wo,
    wt,
    ws,
    arrived,
    bias,
    shifts,
    ext,
    kept,
    sums,
    back,
    weight_sem,
    sent,
    got,
    side_sent,
    side_got,
    rim_sent,
    rim_got,
    back_sent,
    back_got,
    own_sem,
    *,
    n,
):
    channels = latents.shape[-1]
    rows = n * WIDE
    me = lax.axis_index("tm")
    mesh_id = pl.DeviceIdType.MESH

    barrier = pltpu.get_barrier_semaphore()

    @pl.loop(1, n)
    def _(k):
        pl.semaphore_signal(
            barrier, inc=1, device_id={"tm": lax.rem(me + k, n)}, device_id_type=mesh_id
        )

    row, column = place_of(me)
    owns_in = [
        pltpu.make_async_copy(
            latents.at[row * TALL + g, column], arrived.at[g, me], own_sem.at[0, g]
        )
        for g in range(TALL)
    ]
    for copy in owns_in:
        copy.start()
    weights = [
        pltpu.make_async_copy(source, target, weight_sem.at[i])
        for i, (source, target) in enumerate(
            (
                (wq_any, wqkv.at[:, :channels]),
                (wk_any, wqkv.at[:, channels : 2 * channels]),
                (wv_any, wqkv.at[:, 2 * channels :]),
                (wo_any, wo),
                (wt_any.at[0], wt.at[:, :channels]),
                (wt_any.at[1], wt.at[:, channels : 2 * channels]),
                (wt_any.at[2], wt.at[:, 2 * channels :]),
                (ws_any, ws),
            )
        )
    ]
    for copy in weights:
        copy.start()
    pl.semaphore_wait(barrier, n - 1)

    def in_copy(g, k):
        peer = lax.rem(me + n - k, n)
        to_row, to_column = place_of(peer)
        return pltpu.make_async_remote_copy(
            src_ref=latents.at[to_row * TALL + g, to_column],
            dst_ref=arrived.at[g, me],
            send_sem=sent.at[g],
            recv_sem=got.at[g],
            device_id={"tm": peer},
            device_id_type=mesh_id,
        )

    def in_all(g):
        return pltpu.make_async_remote_copy(
            src_ref=arrived.at[g, 1:],
            dst_ref=arrived.at[g, 1:],
            send_sem=sent.at[g],
            recv_sem=got.at[g],
            device_id={"tm": (me + 1) % n},
            device_id_type=mesh_id,
        )

    for g in range(TALL):

        @pl.loop(1, n)
        def _(k):
            in_copy(g, k).start()

    edge = jnp.zeros((n, channels), jnp.bfloat16)

    @pl.when(row == 0)
    def _():
        for i in range(WIDE + 2):
            ext[0, i] = edge

    @pl.when(row == DOWN - 1)
    def _():
        for i in range(WIDE + 2):
            ext[TALL + 1, i] = edge

    @pl.when(column == 0)
    def _():
        for i in range(TALL + 2):
            ext[i, 0] = edge

    @pl.when(column == ACROSS - 1)
    def _():
        for i in range(TALL + 2):
            ext[i, WIDE + 1] = edge

    flat = iota((rows, 1), 0)
    by_position = one_hot((flat % n) * WIDE + flat // n, rows)
    by_frame = one_hot((flat % WIDE) * n + flat // WIDE, rows)

    at, other = iota(bias.shape, 0), iota(bias.shape, 1)
    seen = jnp.logical_and((at & (WIDE - 1)) == (other & (WIDE - 1)), other <= at)
    bias[...] = jnp.where(seen, 0.0, -1e30)

    lanes = shifts.shape[-1]
    frame = iota((rows, lanes), 0) // WIDE
    new_start = jnp.zeros(frame.shape, jnp.int32)
    for t in range(starts.shape[0]):
        new_start = jnp.maximum(new_start, jnp.where(frame >= starts[t], starts[t], 0))
    old_start = jnp.zeros(frame.shape, jnp.int32)
    for t in range(starts.shape[0]):
        old_start = jnp.maximum(old_start, jnp.where(new_start > starts[t], starts[t], 0))
    inside = frame - new_start
    shifts[0] = inside.astype(jnp.float32)
    shifts[1] = (frame - old_start).astype(jnp.float32)
    shifts[2] = jnp.where(
        jnp.logical_and(new_start > 0, inside < OV),
        (inside + 1).astype(jnp.float32) / float(OV + 1),
        jnp.float32(1.0),
    )

    def wide(tile):
        return jnp.concatenate([tile] * (channels // lanes), axis=1)

    def blend(g):
        held = arrived[g].reshape(rows, channels).astype(jnp.float32)
        projected = matmul(normalized(held), wqkv[...]).astype(jnp.bfloat16)
        queries = projected[:, :channels]
        keys = projected[:, channels : 2 * channels]
        values = projected[:, 2 * channels :]
        attended = []
        for low in range(0, rows, rows // PARTS):
            high = low + rows // PARTS
            scores = lax.dot_general(
                queries[low:high],
                keys[:high],
                (((1,), (1,)), ((), ())),
                preferred_element_type=jnp.float32,
            )
            scores = scores * (channels ** (-0.5) * 1.4426950408889634) + bias[low:high, :high]
            expo = jnp.exp2(scores - jnp.max(scores, axis=-1, keepdims=True))
            share = (expo * (1.0 / jnp.sum(expo, axis=-1, keepdims=True))).astype(jnp.bfloat16)
            attended.append(matmul(share, values[:high]).astype(jnp.bfloat16))
        attended = jnp.concatenate(attended, axis=0)
        hidden = (held + matmul(attended, wo[...])).astype(jnp.bfloat16)
        smooth = normalized(hidden.astype(jnp.float32))
        products = matmul(smooth, wt[...])
        current = products[:, :channels]
        none = jnp.zeros((2 * WIDE, channels), jnp.float32)
        lag1 = products[:, channels : 2 * channels]
        lag2 = products[:, 2 * channels :]
        one_back = jnp.concatenate([none[:WIDE], lag1[: rows - WIDE]], axis=0)
        two_one = jnp.concatenate([none[:WIDE], lag2[: rows - WIDE]], axis=0)
        two_back = jnp.concatenate([none, lag2[: rows - 2 * WIDE]], axis=0)

        def mixed(reach):
            one = jnp.where(reach >= 1.0, one_back, lag1)
            two = jnp.where(reach >= 2.0, two_back, jnp.where(reach >= 1.0, two_one, lag2))
            return half_silu(current + one + two)

        fade = wide(shifts[2])
        blended = fade * mixed(wide(shifts[0])) + (1.0 - fade) * mixed(wide(shifts[1]))
        turned = matmul(by_position, blended.astype(jnp.bfloat16)).astype(jnp.bfloat16)
        ext[g + 1, 1 : WIDE + 1] = turned.reshape(WIDE, n, channels)
        return hidden

    def link(down, right, source, target, send_sem, recv_sem):
        to_row, to_column = row + down, column + right
        there = jnp.logical_and(
            jnp.logical_and(to_row >= 0, to_row < DOWN),
            jnp.logical_and(to_column >= 0, to_column < ACROSS),
        )
        from_row, from_column = row - down, column - right
        comes = jnp.logical_and(
            jnp.logical_and(from_row >= 0, from_row < DOWN),
            jnp.logical_and(from_column >= 0, from_column < ACROSS),
        )
        peer = device_at(lax.rem(to_row + DOWN, DOWN), lax.rem(to_column + ACROSS, ACROSS))
        copy = pltpu.make_async_remote_copy(
            src_ref=source,
            dst_ref=target,
            send_sem=send_sem,
            recv_sem=recv_sem,
            device_id={"tm": peer},
            device_id_type=mesh_id,
        )
        return copy, there, comes

    sides = [
        [
            link(0, -1, ext.at[e, 1], ext.at[e, WIDE + 1], side_sent.at[e, 0], side_got.at[e, 0]),
            link(0, 1, ext.at[e, WIDE], ext.at[e, 0], side_sent.at[e, 1], side_got.at[e, 1]),
        ]
        for e in range(1, TALL + 1)
    ]
    inner = pl.ds(1, WIDE)
    rims = [
        [
            link(d, -1, ext.at[e, 1], ext.at[t, WIDE + 1], rim_sent.at[i, 1], rim_got.at[i, 1]),
            link(d, 1, ext.at[e, WIDE], ext.at[t, 0], rim_sent.at[i, 2], rim_got.at[i, 2]),
            link(d, 0, ext.at[e, inner], ext.at[t, inner], rim_sent.at[i, 0], rim_got.at[i, 0]),
        ]
        for i, (d, e, t) in enumerate(((-1, 1, TALL + 1), (1, TALL, 0)))
    ]

    def send(links):
        for copy, there, comes in links:

            @pl.when(there)
            def _():
                copy.start()

    def receive(links):
        for copy, there, comes in links:

            @pl.when(comes)
            def _():
                copy.wait_recv()

    def taps(g, e, columns):
        return sum(
            matmul(ext[e, b : b + WIDE].reshape(rows, channels), ws[e - g, b]) for b in columns
        )

    def back_copy(g, k):
        peer = lax.rem(me + k, n)
        return pltpu.make_async_remote_copy(
            src_ref=back.at[g, peer],
            dst_ref=returned.at[row * TALL + g, column],
            send_sem=back_sent,
            recv_sem=back_got,
            device_id={"tm": peer},
            device_id_type=mesh_id,
        )

    owns_out = [
        pltpu.make_async_copy(
            back.at[g, me], returned.at[row * TALL + g, column], own_sem.at[1, g]
        )
        for g in range(TALL)
    ]

    def finish(g, total):
        total = (kept[g] + total).astype(jnp.bfloat16)
        back[g] = matmul(by_frame, total).astype(jnp.bfloat16).reshape(n, WIDE, channels)

        @pl.loop(1, n)
        def _(k):
            back_copy(g, k).start()

        owns_out[g].start()

    for copy in weights:
        copy.wait()
    for copy in owns_in:
        copy.wait()

    in_all(0).wait_recv()
    hidden = blend(0)
    send(sides[0])
    send(rims[0])
    kept[0] = matmul(by_position, hidden)
    sums[0] = taps(0, 1, (1,))
    sums[1] = taps(1, 1, (1,))

    in_all(1).wait_recv()
    hidden = blend(1)
    send(sides[1])
    send(rims[1])
    kept[1] = matmul(by_position, hidden)
    sums[1] = sums[1] + taps(1, 2, (1,))
    receive(sides[0])
    receive(rims[0])
    sums[1] = sums[1] + taps(1, 1, (0, 2)) + taps(1, 3, (0, 1, 2))
    receive(sides[1])
    finish(1, sums[1] + taps(1, 2, (0, 2)))
    sums[0] = sums[0] + taps(0, 1, (0, 2)) + taps(0, 2, (0, 1, 2))
    receive(rims[1])
    finish(0, sums[0] + taps(0, 0, (0, 1, 2)))

    for g in range(TALL):
        in_all(g).wait_send()

    for links in sides + rims:
        for copy, there, comes in links:

            @pl.when(there)
            def _():
                copy.wait_send()

    for own in owns_out:
        own.wait()
    everything = pltpu.make_async_remote_copy(
        src_ref=back.at[:, 1:],
        dst_ref=back.at[:, 1:],
        send_sem=back_sent,
        recv_sem=back_got,
        device_id={"tm": (me + 1) % n},
        device_id_type=mesh_id,
    )
    everything.wait_send()
    everything.wait_recv()


PARTS = 1


def settle_kernel(source, target, sem):
    copy = pltpu.make_async_copy(source, target, sem)
    copy.start()
    copy.wait()


def block_body(latents, w_query, w_key, w_value, w_out, w_time, w_space, tile_starts):
    n = lax.axis_size("tm")
    channels = latents.shape[-1]
    rows = n * WIDE
    anywhere = pl.BlockSpec(memory_space=pltpu.HBM)
    dma = pltpu.SemaphoreType.DMA
    bf16 = jnp.bfloat16
    spaced = (PH, PW // WIDE, WIDE, channels)
    blocks = pl.pallas_call(
        functools.partial(block_kernel, n=n),
        out_shape=jax.ShapeDtypeStruct(spaced, bf16),
        in_specs=[pl.BlockSpec(memory_space=pltpu.SMEM)] + [anywhere] * 7,
        out_specs=pl.BlockSpec(memory_space=pl.ANY),
        scratch_shapes=[
            pltpu.VMEM((channels, 3 * channels), bf16),
            pltpu.VMEM(w_out.shape, bf16),
            pltpu.VMEM((channels, 3 * channels), bf16),
            pltpu.VMEM(w_space.shape, bf16),
            pltpu.VMEM((TALL, n, WIDE, channels), bf16),
            pltpu.VMEM((rows, rows), jnp.float32),
            pltpu.VMEM((3, rows, 128), jnp.float32),
            pltpu.VMEM((TALL + 2, WIDE + 2, n, channels), bf16),
            pltpu.VMEM((TALL, rows, channels), jnp.float32),
            pltpu.VMEM((TALL, rows, channels), jnp.float32),
            pltpu.VMEM((TALL, n, WIDE, channels), bf16),
            dma((8,)),
            dma((TALL,)),
            dma((TALL,)),
            dma((TALL + 1, 2)),
            dma((TALL + 1, 2)),
            dma((2, 3)),
            dma((2, 3)),
            dma(()),
            dma(()),
            dma((2, TALL)),
        ],
        compiler_params=pltpu.CompilerParams(
            collective_id=0, has_side_effects=True, vmem_limit_bytes=53 * 2**20
        ),
    )(pltpu.with_memory_space_constraint(tile_starts, pltpu.HBM), latents.reshape(spaced), w_query, w_key, w_value, w_out, w_time, w_space)
    settled = pl.pallas_call(
        settle_kernel,
        out_shape=jax.ShapeDtypeStruct(spaced, bf16),
        in_specs=[pl.BlockSpec(memory_space=pl.ANY)],
        out_specs=anywhere,
        scratch_shapes=[dma(())],
        compiler_params=pltpu.CompilerParams(vmem_limit_bytes=2**20),
    )(blocks)
    return settled.reshape(latents.shape)


def any_body(latents, *rest):
    frames_dev, row_count, channels = latents.shape
    fits = row_count == PH * PW and PH == TALL * DOWN and PW == WIDE * ACROSS
    if frames_dev == 1 and lax.axis_size("tm") == DOWN * ACROSS and fits:
        return block_body(latents, *rest)
    return body(latents, *rest)


def solution(mesh):
    placed = (P(("groups", "tm"), None, None), P(), P(), P(), P(), P(), P(), P("groups"))
    return jax.shard_map(
        any_body, mesh=mesh, in_specs=placed, out_specs=P(("groups", "tm"), None, None), check_vma=False
    )
```

```python
import functools

import jax
import jax.numpy as jnp
from jax import lax
from jax.experimental import pallas as pl
from jax.experimental.pallas import tpu as pltpu
from jax.sharding import PartitionSpec as P

PH = 16
PW = 32
OV = 2


epsilon = 1e-06


def passed_along(block, axis, distance):
    devices = range(lax.axis_size(axis))
    route = [(i - distance, i) for i in devices if i - distance in devices]
    return lax.ppermute(block, axis, route)


def rms_norm(array):
    wide = array.astype(jnp.float32)
    return (wide * lax.rsqrt(jnp.mean(wide * wide, axis=-1, keepdims=True) + epsilon)).astype(
        jnp.bfloat16
    )


def project(array, weight):
    extent = array.shape
    product = jnp.dot(array.reshape(-1, extent[-1]), weight, preferred_element_type=jnp.float32)
    return product.reshape(extent[:-1] + (weight.shape[-1],))


def tile_frames(frames, starts):
    reached = starts[None, :] <= frames[:, None]
    new_start = jnp.max(jnp.where(reached, starts[None, :], 0), axis=1)
    earlier = starts[None, :] < new_start[:, None]
    old_start = jnp.max(jnp.where(earlier, starts[None, :], 0), axis=1)
    inside = frames - new_start
    shared = jnp.logical_and(new_start > 0, inside < OV)
    fade = jnp.where(shared, (inside + 1).astype(jnp.float32) / float(OV + 1), jnp.float32(1.0))
    return (new_start, old_start, fade[:, None, None])


def attend(triple):
    queries, key_rows, values = triple
    length = queries.shape[0]
    scale = queries.shape[-1] ** (-0.5)
    scores = (
        jnp.einsum("fipc,gipc->ipfg", queries, key_rows, preferred_element_type=jnp.float32) * scale
    )
    order = jnp.arange(length)
    causal = order[:, None] >= order[None, :]
    scores = jnp.where(causal[None, None], scores, jnp.float32(-1e30))
    peak = jnp.max(scores, axis=-1, keepdims=True)
    expo = jnp.exp(scores - peak)
    weights = (expo / jnp.sum(expo, axis=-1, keepdims=True)).astype(jnp.bfloat16)
    return jnp.einsum(
        "ipfg,gipc->fipc", weights, values, preferred_element_type=jnp.float32
    ).astype(jnp.bfloat16)


def time_blend(padded, frames, starts, w_time):
    length = frames.shape[0]
    extent = padded.shape
    channels = extent[-1]
    flattened = padded.reshape(-1, channels)
    products = [
        jnp.dot(flattened, w_time[lag_index], preferred_element_type=jnp.float32).reshape(
            extent[0], -1, channels
        )
        for lag_index in range(3)
    ]
    new_start, old_start, fade = tile_frames(frames, starts)

    def mixed(context):
        summed = jnp.zeros((length,) + products[0].shape[1:], jnp.float32)
        for lag_index in range(3):
            actual = jnp.minimum(lag_index, frames - context)
            for delta_back in range(lag_index + 1):
                chosen = (actual == delta_back).astype(jnp.float32)[:, None, None]
                summed = (
                    summed + chosen * products[lag_index][2 - delta_back : 2 - delta_back + length]
                )
        return summed

    blended = fade * jax.nn.silu(mixed(new_start)) + (1.0 - fade) * jax.nn.silu(mixed(old_start))
    return blended.astype(jnp.bfloat16)


def space_mix(blended, hidden, w_space):
    length = blended.shape[0]
    channels = blended.shape[-1]
    spatial = blended.reshape(length, PH, PW, channels)
    padded = jnp.pad(spatial, ((0, 0), (1, 1), (1, 1), (0, 0)))
    summed = hidden.reshape(-1, channels).astype(jnp.float32)
    for row_shift in range(3):
        for col_shift in range(3):
            window = padded[:, row_shift : row_shift + PH, col_shift : col_shift + PW].reshape(
                -1, channels
            )
            summed = summed + jnp.dot(
                window, w_space[row_shift, col_shift], preferred_element_type=jnp.float32
            )
    return summed.reshape(length, PH * PW, channels).astype(jnp.bfloat16)


def body(latents, w_query, w_key, w_value, w_out, w_time, w_space, tile_starts):
    frames_dev, row_count, channels = latents.shape
    devices_tm = lax.axis_size("tm")
    share = row_count // devices_tm
    normed = rms_norm(latents).reshape(frames_dev, devices_tm, share, channels)
    queries = project(normed, w_query).astype(jnp.bfloat16)
    key_rows = project(normed, w_key).astype(jnp.bfloat16)
    values = project(normed, w_value).astype(jnp.bfloat16)
    attended = attend(
        (
            lax.all_to_all(queries, "tm", split_axis=1, concat_axis=0, tiled=True),
            lax.all_to_all(key_rows, "tm", split_axis=1, concat_axis=0, tiled=True),
            lax.all_to_all(values, "tm", split_axis=1, concat_axis=0, tiled=True),
        )
    )
    attended = lax.all_to_all(attended, "tm", split_axis=0, concat_axis=1, tiled=True).reshape(
        frames_dev, row_count, channels
    )
    hidden = (latents.astype(jnp.float32) + project(attended, w_out)).astype(jnp.bfloat16)
    smooth = rms_norm(hidden)
    reach = (frames_dev + 1) // frames_dev
    pieces = [passed_along(smooth, "tm", stride) for stride in range(reach, 0, -1)]
    earlier = jnp.concatenate(pieces, axis=0)
    offset = lax.axis_index("tm") * frames_dev
    frames = offset + jnp.arange(frames_dev)
    blended = time_blend(jnp.concatenate([earlier, smooth], axis=0), frames, tile_starts, w_time)
    return space_mix(blended, hidden, w_space)


TALL = 2
WIDE = 8
DOWN = 8
ACROSS = 4


def iota(shape, dim):
    return lax.broadcasted_iota(jnp.int32, shape, dim)


def one_hot(target, columns):
    rows = target.shape[0]
    return (jnp.broadcast_to(target, (rows, columns)) == iota((rows, columns), 1)).astype(
        jnp.float32
    ).astype(jnp.bfloat16)


def matmul(left, right):
    return jnp.dot(left, right, preferred_element_type=jnp.float32)


def place_of(device):
    core, x = lax.rem(device, 2), lax.rem(lax.div(device, 2), 2)
    y, z = lax.rem(lax.div(device, 4), 2), lax.div(device, 8)
    return 2 * z + lax.rem(core + z, 2), 2 * y + lax.rem(x + y, 2)


def device_at(row, column):
    z, y = lax.div(row, 2), lax.div(column, 2)
    return z * 8 + y * 4 + lax.rem(column + y, 2) * 2 + lax.rem(row + z, 2)


def normalized(wide):
    scale = lax.rsqrt(jnp.mean(wide * wide, axis=-1, keepdims=True) + epsilon)
    return (wide * scale).astype(jnp.bfloat16)


def half_silu(v):
    half = 0.5 * v
    return half + half * jnp.tanh(half)


def block_kernel(
    starts,
    latents,
    wq_any,
    wk_any,
    wv_any,
    wo_any,
    wt_any,
    ws_any,
    returned,
    staged,
    wqkv,
    wo,
    wt,
    ws,
    arrived,
    bias,
    shifts,
    ext,
    kept,
    sums,
    back,
    weight_sem,
    sent,
    got,
    side_sent,
    side_got,
    rim_sent,
    rim_got,
    back_sent,
    back_got,
    own_sem,
    *,
    n,
):
    channels = latents.shape[-1]
    rows = n * WIDE
    me = lax.axis_index("tm")
    mesh_id = pl.DeviceIdType.MESH

    barrier = pltpu.get_barrier_semaphore()

    @pl.loop(1, n)
    def _(k):
        pl.semaphore_signal(
            barrier, inc=1, device_id={"tm": lax.rem(me + k, n)}, device_id_type=mesh_id
        )

    fetch = pltpu.make_async_copy(latents, staged, weight_sem.at[8])
    fetch.start()
    row, column = place_of(me)
    owns_in = [
        pltpu.make_async_copy(
            latents.at[row * TALL + g, column], arrived.at[g, me], own_sem.at[0, g]
        )
        for g in range(TALL)
    ]
    for copy in owns_in:
        copy.start()
    weights = [
        pltpu.make_async_copy(source, target, weight_sem.at[i])
        for i, (source, target) in enumerate(
            (
                (wq_any, wqkv.at[:, :channels]),
                (wk_any, wqkv.at[:, channels : 2 * channels]),
                (wv_any, wqkv.at[:, 2 * channels :]),
                (wo_any, wo),
                (wt_any.at[0], wt.at[:, :channels]),
                (wt_any.at[1], wt.at[:, channels : 2 * channels]),
                (wt_any.at[2], wt.at[:, 2 * channels :]),
                (ws_any, ws),
            )
        )
    ]
    for copy in weights[:3]:
        copy.start()
    fetch.wait()
    pl.semaphore_wait(barrier, n - 1)

    def in_copy(g, k):
        peer = lax.rem(me + n - k, n)
        to_row, to_column = place_of(peer)
        return pltpu.make_async_remote_copy(
            src_ref=staged.at[to_row * TALL + g, to_column],
            dst_ref=arrived.at[g, me],
            send_sem=sent.at[g],
            recv_sem=got.at[g],
            device_id={"tm": peer},
            device_id_type=mesh_id,
        )

    def in_all(g):
        return pltpu.make_async_remote_copy(
            src_ref=arrived.at[g, 1:],
            dst_ref=arrived.at[g, 1:],
            send_sem=sent.at[g],
            recv_sem=got.at[g],
            device_id={"tm": (me + 1) % n},
            device_id_type=mesh_id,
        )

    for g in range(TALL):

        @pl.loop(1, n)
        def _(k):
            in_copy(g, k).start()

    for copy in weights[3:]:
        copy.start()

    edge = jnp.zeros((n, channels), jnp.bfloat16)

    @pl.when(row == 0)
    def _():
        for i in range(WIDE + 2):
            ext[0, i] = edge

    @pl.when(row == DOWN - 1)
    def _():
        for i in range(WIDE + 2):
            ext[TALL + 1, i] = edge

    @pl.when(column == 0)
    def _():
        for i in range(TALL + 2):
            ext[i, 0] = edge

    @pl.when(column == ACROSS - 1)
    def _():
        for i in range(TALL + 2):
            ext[i, WIDE + 1] = edge

    flat = iota((rows, 1), 0)
    by_position = one_hot((flat % n) * WIDE + flat // n, rows)
    by_frame = one_hot((flat % WIDE) * n + flat // WIDE, rows)

    at, other = iota(bias.shape, 0), iota(bias.shape, 1)
    seen = jnp.logical_and((at & (WIDE - 1)) == (other & (WIDE - 1)), other <= at)
    bias[...] = jnp.where(seen, 0.0, -1e30)

    lanes = shifts.shape[-1]
    frame = iota((rows, lanes), 0) // WIDE
    new_start = jnp.zeros(frame.shape, jnp.int32)
    for t in range(starts.shape[0]):
        new_start = jnp.maximum(new_start, jnp.where(frame >= starts[t], starts[t], 0))
    old_start = jnp.zeros(frame.shape, jnp.int32)
    for t in range(starts.shape[0]):
        old_start = jnp.maximum(old_start, jnp.where(new_start > starts[t], starts[t], 0))
    inside = frame - new_start
    shifts[0] = inside.astype(jnp.float32)
    shifts[1] = (frame - old_start).astype(jnp.float32)
    shifts[2] = jnp.where(
        jnp.logical_and(new_start > 0, inside < OV),
        (inside + 1).astype(jnp.float32) / float(OV + 1),
        jnp.float32(1.0),
    )

    def wide(tile):
        return jnp.concatenate([tile] * (channels // lanes), axis=1)

    def blend(g):
        held = arrived[g].reshape(rows, channels).astype(jnp.float32)
        projected = matmul(normalized(held), wqkv[...]).astype(jnp.bfloat16)
        queries = projected[:, :channels]
        keys = projected[:, channels : 2 * channels]
        values = projected[:, 2 * channels :]
        attended = []
        for low in range(0, rows, rows // PARTS):
            high = low + rows // PARTS
            scores = lax.dot_general(
                queries[low:high],
                keys[:high],
                (((1,), (1,)), ((), ())),
                preferred_element_type=jnp.float32,
            )
            scores = scores * (channels ** (-0.5) * 1.4426950408889634) + bias[low:high, :high]
            expo = jnp.exp2(scores - jnp.max(scores, axis=-1, keepdims=True))
            share = (expo * (1.0 / jnp.sum(expo, axis=-1, keepdims=True))).astype(jnp.bfloat16)
            attended.append(matmul(share, values[:high]).astype(jnp.bfloat16))
        attended = jnp.concatenate(attended, axis=0)
        hidden = (held + matmul(attended, wo[...])).astype(jnp.bfloat16)
        smooth = normalized(hidden.astype(jnp.float32))
        products = matmul(smooth, wt[...])
        current = products[:, :channels]
        none = jnp.zeros((2 * WIDE, channels), jnp.float32)
        lag1 = products[:, channels : 2 * channels]
        lag2 = products[:, 2 * channels :]
        one_back = jnp.concatenate([none[:WIDE], lag1[: rows - WIDE]], axis=0)
        two_one = jnp.concatenate([none[:WIDE], lag2[: rows - WIDE]], axis=0)
        two_back = jnp.concatenate([none, lag2[: rows - 2 * WIDE]], axis=0)

        def mixed(reach):
            one = jnp.where(reach >= 1.0, one_back, lag1)
            two = jnp.where(reach >= 2.0, two_back, jnp.where(reach >= 1.0, two_one, lag2))
            return half_silu(current + one + two)

        fade = wide(shifts[2])
        blended = fade * mixed(wide(shifts[0])) + (1.0 - fade) * mixed(wide(shifts[1]))
        turned = matmul(by_position, blended.astype(jnp.bfloat16)).astype(jnp.bfloat16)
        ext[g + 1, 1 : WIDE + 1] = turned.reshape(WIDE, n, channels)
        return hidden

    def link(down, right, source, target, send_sem, recv_sem):
        to_row, to_column = row + down, column + right
        there = jnp.logical_and(
            jnp.logical_and(to_row >= 0, to_row < DOWN),
            jnp.logical_and(to_column >= 0, to_column < ACROSS),
        )
        from_row, from_column = row - down, column - right
        comes = jnp.logical_and(
            jnp.logical_and(from_row >= 0, from_row < DOWN),
            jnp.logical_and(from_column >= 0, from_column < ACROSS),
        )
        peer = device_at(lax.rem(to_row + DOWN, DOWN), lax.rem(to_column + ACROSS, ACROSS))
        copy = pltpu.make_async_remote_copy(
            src_ref=source,
            dst_ref=target,
            send_sem=send_sem,
            recv_sem=recv_sem,
            device_id={"tm": peer},
            device_id_type=mesh_id,
        )
        return copy, there, comes

    sides = [
        [
            link(0, -1, ext.at[e, 1], ext.at[e, WIDE + 1], side_sent.at[e, 0], side_got.at[e, 0]),
            link(0, 1, ext.at[e, WIDE], ext.at[e, 0], side_sent.at[e, 1], side_got.at[e, 1]),
        ]
        for e in range(1, TALL + 1)
    ]
    inner = pl.ds(1, WIDE)
    rims = [
        [
            link(d, -1, ext.at[e, 1], ext.at[t, WIDE + 1], rim_sent.at[i, 1], rim_got.at[i, 1]),
            link(d, 1, ext.at[e, WIDE], ext.at[t, 0], rim_sent.at[i, 2], rim_got.at[i, 2]),
            link(d, 0, ext.at[e, inner], ext.at[t, inner], rim_sent.at[i, 0], rim_got.at[i, 0]),
        ]
        for i, (d, e, t) in enumerate(((-1, 1, TALL + 1), (1, TALL, 0)))
    ]

    def send(links):
        for copy, there, comes in links:

            @pl.when(there)
            def _():
                copy.start()

    def receive(links):
        for copy, there, comes in links:

            @pl.when(comes)
            def _():
                copy.wait_recv()

    def taps(g, e, columns):
        return sum(
            matmul(ext[e, b : b + WIDE].reshape(rows, channels), ws[e - g, b]) for b in columns
        )

    def back_copy(g, k):
        peer = lax.rem(me + k, n)
        return pltpu.make_async_remote_copy(
            src_ref=back.at[g, peer],
            dst_ref=returned.at[row * TALL + g, column],
            send_sem=back_sent,
            recv_sem=back_got,
            device_id={"tm": peer},
            device_id_type=mesh_id,
        )

    owns_out = [
        pltpu.make_async_copy(
            back.at[g, me], returned.at[row * TALL + g, column], own_sem.at[1, g]
        )
        for g in range(TALL)
    ]

    def finish(g, total):
        total = (kept[g] + total).astype(jnp.bfloat16)
        back[g] = matmul(by_frame, total).astype(jnp.bfloat16).reshape(n, WIDE, channels)

        @pl.loop(1, n)
        def _(k):
            back_copy(g, k).start()

        owns_out[g].start()

    for copy in weights:
        copy.wait()
    for copy in owns_in:
        copy.wait()

    in_all(0).wait_recv()
    hidden = blend(0)
    send(sides[0])
    send(rims[0])
    kept[0] = matmul(by_position, hidden)
    sums[0] = taps(0, 1, (1,))
    sums[1] = taps(1, 1, (1,))

    in_all(1).wait_recv()
    hidden = blend(1)
    send(sides[1])
    send(rims[1])
    kept[1] = matmul(by_position, hidden)
    sums[1] = sums[1] + taps(1, 2, (1,))
    receive(sides[0])
    receive(rims[0])
    sums[1] = sums[1] + taps(1, 1, (0, 2)) + taps(1, 3, (0, 1, 2))
    receive(sides[1])
    finish(1, sums[1] + taps(1, 2, (0, 2)))
    sums[0] = sums[0] + taps(0, 1, (0, 2)) + taps(0, 2, (0, 1, 2))
    receive(rims[1])
    finish(0, sums[0] + taps(0, 0, (0, 1, 2)))

    for g in range(TALL):
        in_all(g).wait_send()

    for links in sides + rims:
        for copy, there, comes in links:

            @pl.when(there)
            def _():
                copy.wait_send()

    for own in owns_out:
        own.wait()
    everything = pltpu.make_async_remote_copy(
        src_ref=back.at[:, 1:],
        dst_ref=back.at[:, 1:],
        send_sem=back_sent,
        recv_sem=back_got,
        device_id={"tm": (me + 1) % n},
        device_id_type=mesh_id,
    )
    everything.wait_send()
    everything.wait_recv()


PARTS = 1


def settle_kernel(source, target, sem):
    copy = pltpu.make_async_copy(source, target, sem)
    copy.start()
    copy.wait()


def block_body(latents, w_query, w_key, w_value, w_out, w_time, w_space, tile_starts):
    n = lax.axis_size("tm")
    channels = latents.shape[-1]
    rows = n * WIDE
    anywhere = pl.BlockSpec(memory_space=pltpu.HBM)
    dma = pltpu.SemaphoreType.DMA
    bf16 = jnp.bfloat16
    spaced = (PH, PW // WIDE, WIDE, channels)
    blocks = pl.pallas_call(
        functools.partial(block_kernel, n=n),
        out_shape=jax.ShapeDtypeStruct(spaced, bf16),
        in_specs=[pl.BlockSpec(memory_space=pltpu.SMEM)] + [anywhere] * 7,
        out_specs=pl.BlockSpec(memory_space=pl.ANY),
        scratch_shapes=[
            pltpu.VMEM(spaced, bf16),
            pltpu.VMEM((channels, 3 * channels), bf16),
            pltpu.VMEM(w_out.shape, bf16),
            pltpu.VMEM((channels, 3 * channels), bf16),
            pltpu.VMEM(w_space.shape, bf16),
            pltpu.VMEM((TALL, n, WIDE, channels), bf16),
            pltpu.VMEM((rows, rows), jnp.float32),
            pltpu.VMEM((3, rows, 128), jnp.float32),
            pltpu.VMEM((TALL + 2, WIDE + 2, n, channels), bf16),
            pltpu.VMEM((TALL, rows, channels), jnp.float32),
            pltpu.VMEM((TALL, rows, channels), jnp.float32),
            pltpu.VMEM((TALL, n, WIDE, channels), bf16),
            dma((9,)),
            dma((TALL,)),
            dma((TALL,)),
            dma((TALL + 1, 2)),
            dma((TALL + 1, 2)),
            dma((2, 3)),
            dma((2, 3)),
            dma(()),
            dma(()),
            dma((2, TALL)),
        ],
        compiler_params=pltpu.CompilerParams(
            collective_id=0, has_side_effects=True, vmem_limit_bytes=53 * 2**20
        ),
    )(pltpu.with_memory_space_constraint(tile_starts, pltpu.HBM), latents.reshape(spaced), w_query, w_key, w_value, w_out, w_time, w_space)
    settled = pl.pallas_call(
        settle_kernel,
        out_shape=jax.ShapeDtypeStruct(spaced, bf16),
        in_specs=[pl.BlockSpec(memory_space=pl.ANY)],
        out_specs=anywhere,
        scratch_shapes=[dma(())],
        compiler_params=pltpu.CompilerParams(vmem_limit_bytes=2**20),
    )(blocks)
    return settled.reshape(latents.shape)


def any_body(latents, *rest):
    frames_dev, row_count, channels = latents.shape
    fits = row_count == PH * PW and PH == TALL * DOWN and PW == WIDE * ACROSS
    if frames_dev == 1 and lax.axis_size("tm") == DOWN * ACROSS and fits:
        return block_body(latents, *rest)
    return body(latents, *rest)


def solution(mesh):
    placed = (P(("groups", "tm"), None, None), P(), P(), P(), P(), P(), P(), P("groups"))
    return jax.shard_map(
        any_body, mesh=mesh, in_specs=placed, out_specs=P(("groups", "tm"), None, None), check_vma=False
    )
```
